256 devices in a mesh: tm: 64 (over z_hi, y, x), chan: 4 (over z_lo, core).
Axes of the slice: x: 4, y: 4, z: 8 (z_hi: 4, z_lo: 2; z = z_hi * 2 + z_lo), core: 2. Of those that a mesh axis runs over, the one named last changes fastest.
Arguments:
- record: bfloat16 [2048, 32768], P('chan', 'tm')
- event_stretch: int32 [4, 2], replicated, may hold values from 0 to 63
- event_offset: int32 [4, 2], replicated, may hold values from 0 to 12
Outputs:
- scores: float32 [4, 2, 32768], P(None, None, 'tm')
The draws below stay inside these ranges and needn't reach their ends.
Inputs may be any that keep to these rules, and one draw needn't show every extreme that they name: A template lies inside one stretch: event_offset + 500 <= 512.
All inputs are finite; a program needn't handle non-finite values.
Results may differ from the reference program's by a relative error of at most 0.0003.
Values may be sent and summed in bfloat16 or wider, within the bound.
A program may use at most 64 MiB of HBM per device.

```python
import math
import jax
import jax.numpy as jnp
from jax import lax

CHANNELS = 2048
TAPS = 500
STEPS = 4
T_DEV = 512
STRETCHES = 64
SAMPLES = 32768


def draw_record(key, part):
    first, second, third = jax.random.split(key, 3)
    base = jax.random.normal(first, (CHANNELS, SAMPLES), jnp.float32)
    chan_scale = jnp.exp(jax.random.uniform(second, (CHANNELS, 1), jnp.float32, 0.0, math.log(10.0)))
    time_scale = jnp.exp(jax.random.uniform(third, (1, SAMPLES), jnp.float32, 0.0, math.log(4.0)))
    return (0.25 * base * chan_scale * time_scale).astype(jnp.bfloat16)


def set_ends(values, stream_key, low, top_value):
    extent = values.shape
    spot = [jax.random.randint(jax.random.fold_in(stream_key, axis), (), 0, extent[axis]) for axis in range(len(extent))]
    values = values.at[tuple(spot)].set(low)
    longest = extent.index(max(extent))
    spot[longest] = (spot[longest] + 1) % extent[longest]
    return values.at[tuple(spot)].set(top_value)


def setup_inputs(seed: int = 0) -> dict:
    key_list = jax.random.split(jax.random.key(seed), 4)
    return {
        "record": draw_record(jax.random.fold_in(key_list[3], 71), 0),
        "event_stretch": set_ends(jax.random.randint(key_list[1], (STEPS, 2), 0, STRETCHES), jax.random.fold_in(key_list[1], 1), 0, STRETCHES - 1).astype(jnp.int32),
        "event_offset": set_ends(jax.random.randint(key_list[2], (STEPS, 2), 0, T_DEV - TAPS + 1), jax.random.fold_in(key_list[2], 1), 0, T_DEV - TAPS).astype(jnp.int32),
    }


def slide(power, taps, span):
    total = jnp.concatenate([jnp.zeros((1,), jnp.float32), jnp.cumsum(power)])
    return total[taps:taps + span] - total[:span]

def diagonal(product, span):
    count, taps, width = product.shape
    flat = product.reshape(count, taps * width)
    flat = jnp.pad(flat, ((0, 0), (0, taps)))
    return flat.reshape(count, taps, width + 1)[:, :, :span].sum(1)

def reference(record, event_stretch, event_offset):
    padded = jnp.pad(record, ((0, 0), (0, TAPS - 1)))
    starts = (event_stretch * T_DEV + event_offset).astype(jnp.int32)
    pieces = []
    for step in range(STEPS):
        for which in range(2):
            pieces.append(lax.dynamic_slice(record, (jnp.int32(0), starts[step, which]), (CHANNELS, TAPS)))
    templates = jnp.stack(pieces).reshape(STEPS, 2, CHANNELS, TAPS)
    wide = templates.astype(jnp.float32)
    norms = lax.optimization_barrier(jnp.sum(wide * wide, axis=(2, 3)))

    def block(index):
        begin = (index * T_DEV).astype(jnp.int32)
        window = lax.dynamic_slice(padded, (jnp.int32(0), begin), (CHANNELS, T_DEV + TAPS - 1)).astype(jnp.float32)
        power = lax.optimization_barrier(jnp.sum(window * window, axis=0))
        energy = slide(power, TAPS, T_DEV)
        product = jnp.einsum('sjck,cr->sjkr', wide, window)
        corr = diagonal(product.reshape(STEPS * 2, TAPS, T_DEV + TAPS - 1), T_DEV).reshape(STEPS, 2, T_DEV)
        return corr / jnp.sqrt(energy[None, None, :] * norms[:, :, None] + 1e-06)
    blocks = lax.map(block, jnp.arange(STRETCHES, dtype=jnp.int32))
    return jnp.transpose(blocks, (1, 2, 0, 3)).reshape(STEPS, 2, SAMPLES)
```

```python
import functools
import itertools

import jax
import jax.numpy as jnp
from jax import lax
from jax.experimental import pallas as pl
from jax.experimental.pallas import tpu as pltpu
from jax.sharding import Mesh
from jax.sharding import PartitionSpec as P

TAPS = 500
AXES = ("zh", "y", "x", "zl", "core")
SIZE = {"zh": 4, "y": 4, "x": 4, "zl": 2, "core": 2}
MESH = pl.DeviceIdType.MESH
F32 = jnp.float32
BF16 = jnp.bfloat16
SPAN = 512
PLANE = 16
CH = 32
EVENTS = 8
SUB = 32
CHUNK = 2048
WIDE = SPAN + 128


def steps(axes):
    grid = itertools.product(*[range(SIZE[a]) for a in axes])
    return [dict(zip(axes, at)) for at in grid if any(at)]


def moved(me, by, sign=1):
    return {a: lax.rem(me[a] + sign * by[a] + SIZE[a], SIZE[a]) for a in by}


def spot(at, axes):
    index = 0
    for a in axes:
        index = index * SIZE[a] + at[a]
    return index


def remote(src, dst, send, recv, to):
    return pltpu.make_async_remote_copy(
        src_ref=src, dst_ref=dst, send_sem=send, recv_sem=recv, device_id=to, device_id_type=MESH
    )


def greet(me, groups):
    barrier = pltpu.get_barrier_semaphore()
    count = 0
    for axes in groups:
        for by in steps(axes):
            pl.semaphore_signal(barrier, inc=1, device_id=moved(me, by), device_id_type=MESH)
            count += 1
    pl.semaphore_wait(barrier, count)


def exchange_kernel(
    where_ref, x_ref, rec_ref, next_ref, tmpl_ref, cand, picks, s_xy, r_xy, s_z, r_z, s_g, r_g, s_h, r_h, own
):
    me = {a: lax.axis_index(a) for a in AXES}
    greet(me, [("y", "x"), ("zh",)])
    here = spot(me, ("y", "x"))
    zh = me["zh"]
    flat = steps(("y", "x"))
    out = []
    for by in flat:
        to = moved(me, by)
        there = spot(to, ("y", "x"))
        copy = remote(x_ref.at[there], rec_ref.at[here], s_xy.at[there], r_xy.at[here], to)
        copy.start()
        out.append(copy)
    keep = pltpu.make_async_copy(x_ref.at[here], rec_ref.at[here], own)
    keep.start()
    keep.wait()
    for by in flat:
        source = moved(me, by, -1)
        there = spot(source, ("y", "x"))
        remote(x_ref.at[there], rec_ref.at[there], s_xy.at[there], r_xy.at[there], source).wait_recv()

    for j in range(EVENTS):
        cand[j // 2, j % 2] = rec_ref[lax.rem(where_ref[j], PLANE)]
    back = {"zh": lax.rem(zh + 3, 4)}
    for d in (2, 1, 3):
        to = {"zh": lax.rem(zh + d, 4)}
        copy = remote(cand.at[to["zh"]], picks.at[zh], s_z.at[to["zh"]], r_z.at[zh], to)
        copy.start()
        out.append(copy)
    halo = remote(rec_ref.at[0], next_ref, s_h, r_h, back)
    halo.start()
    picks[zh] = cand[zh]
    for d in (1, 2, 3):
        q = lax.rem(zh + d, 4)
        remote(cand.at[q], picks.at[q], s_z.at[q], r_z.at[q], {"zh": q}).wait_recv()

    for i in range(2):
        tmpl_ref[zh, i] = picks[lax.div(where_ref[2 * zh + i], PLANE), i]
    for d in (2, 1, 3):
        to = {"zh": lax.rem(zh + d, 4)}
        copy = remote(tmpl_ref.at[zh], tmpl_ref.at[zh], s_g.at[to["zh"]], r_g.at[zh], to)
        copy.start()
        out.append(copy)
    for d in (1, 2, 3):
        q = lax.rem(zh + d, 4)
        remote(tmpl_ref.at[q], tmpl_ref.at[q], s_g.at[q], r_g.at[q], {"zh": q}).wait_recv()
    halo.wait()
    for copy in out:
        copy.wait_send()


def exchange(where, record):
    dma = pltpu.SemaphoreType.DMA
    return pl.pallas_call(
        exchange_kernel,
        out_shape=(
            jax.ShapeDtypeStruct((PLANE, CH, SPAN), BF16),
            jax.ShapeDtypeStruct((CH, SPAN), BF16),
            jax.ShapeDtypeStruct((4, 2, CH, SPAN), BF16),
        ),
        in_specs=[pl.BlockSpec(memory_space=pltpu.SMEM), pl.BlockSpec(memory_space=pl.ANY)],
        out_specs=(pl.BlockSpec(memory_space=pltpu.VMEM),) * 3,
        scratch_shapes=[
            pltpu.VMEM((4, 2, CH, SPAN), BF16),
            pltpu.VMEM((4, 2, CH, SPAN), BF16),
            dma((PLANE,)),
            dma((PLANE,)),
            dma((4,)),
            dma((4,)),
            dma((4,)),
            dma((4,)),
            dma,
            dma,
            dma,
        ],
        compiler_params=pltpu.CompilerParams(collective_id=0, has_side_effects=True),
        name="exchange",
    )(where, record.reshape(PLANE, CH, SPAN))


def left(x, by):
    return pltpu.roll(x, x.shape[1] - by, 1) if by else x


def correlate_kernel(info_ref, rec_ref, next_ref, tmpl_ref, out_ref, phases, taps, product, power):
    lane = lax.broadcasted_iota(jnp.int32, (CH, 128), 1)
    tap = lax.broadcasted_iota(jnp.int32, (CH, SPAN), 1)
    last = info_ref[EVENTS] == 3

    shifted = []
    norms = []
    for j in range(EVENTS):
        wide = pltpu.roll(tmpl_ref[j // 2, j % 2].astype(F32), SPAN - info_ref[j], 1)
        wide = jnp.where(tap < TAPS, wide, 0.0)
        norms.append(jnp.sum(wide * wide, keepdims=True))
        shifted.append(wide)
    for half in range(2):
        for m in range(4):
            for p in range(4):
                tile = jnp.zeros((CH, 128), F32)
                for i in range(4):
                    piece = shifted[4 * half + i][:, 128 * m : 128 * m + 128]
                    tile = jnp.where(lane // SUB == i, left(piece, SUB * (p - i) % 128), tile)
                row = (4 * m + p) * CH
                taps[row : row + CH, 128 * half : 128 * half + 128] = tile.astype(BF16)
    row = lax.broadcasted_iota(jnp.int32, (256, 256), 0)
    col = lax.broadcasted_iota(jnp.int32, (256, 256), 1)
    order = (lax.rem(row, 8) * SUB + lax.div(row, 8) == col).astype(F32).astype(BF16)
    weights = lax.dot_general(
        order, taps[...], (((1,), (1,)), ((), ())), preferred_element_type=F32
    ).astype(BF16)

    def fill(s, here, after):
        power[pl.ds(s, 1), :] = jnp.sum(here * here, axis=0, keepdims=True)
        joined = jnp.concatenate([here, after], axis=1)
        at = pl.multiple_of(s * SPAN, SPAN)
        for p in range(4):
            phases[p * CH : p * CH + CH, pl.ds(at, SPAN)] = left(joined, SUB * p)[:, :SPAN].astype(BF16)

    def halo():
        return jnp.where(last, 0.0, next_ref[...].astype(F32))

    @pl.loop(0, PLANE - 1)
    def _(s):
        fill(s, rec_ref[s].astype(F32), rec_ref[s + 1, :, 0:128].astype(F32))

    fill(PLANE - 1, rec_ref[PLANE - 1].astype(F32), halo()[:, 0:128])
    fill(PLANE, halo(), jnp.zeros((CH, 128), F32))

    double = jnp.concatenate([power[0:PLANE, :], power[1 : PLANE + 1, :]], axis=1)
    sums = {1: double}
    for size in (1, 2, 4, 8, 16, 32, 64, 128):
        sums[2 * size] = sums[size] + left(sums[size], size)
    energy = sums[256][:, :SPAN]
    start = 256
    for size in (128, 64, 32, 16, 4):
        energy = energy + left(sums[size], start)[:, :SPAN]
        start += size

    spread = lax.broadcasted_iota(jnp.int32, (1, 128), 1)
    norm_row = jnp.zeros((1, 128), F32)
    for j in range(EVENTS):
        norm_row = jnp.where(spread == j, norms[j], norm_row)

    for s in range(PLANE):
        for i in range(4):
            out_ref[s, i : i + 1, SPAN:WIDE] = energy[s : s + 1, 128 * i : 128 * i + 128]
        out_ref[s, 4:5, SPAN:WIDE] = norm_row
        out_ref[s, 5:8, SPAN:WIDE] = jnp.zeros((3, 128), F32)

    @pl.loop(0, PLANE * SPAN // CHUNK)
    def _(c):
        at = pl.multiple_of(c * CHUNK, CHUNK)
        stack = jnp.concatenate([phases[:, pl.ds(at + 128 * m, CHUNK + 128)] for m in range(4)], axis=0)
        product[...] = jnp.dot(weights, stack, preferred_element_type=F32)
        total = product[0:8, 0:CHUNK]
        for b in range(1, SUB):
            total = total + left(product[8 * b : 8 * b + 8, :], b)[:, :CHUNK]
        for q in range(CHUNK // SPAN):
            out_ref[c * (CHUNK // SPAN) + q, :, 0:SPAN] = total[:, SPAN * q : SPAN * q + SPAN]


def correlate(info, record, follower, templates):
    return pl.pallas_call(
        correlate_kernel,
        out_shape=jax.ShapeDtypeStruct((PLANE, EVENTS, WIDE), F32),
        in_specs=[pl.BlockSpec(memory_space=pltpu.SMEM)] + [pl.BlockSpec(memory_space=pltpu.VMEM)] * 3,
        out_specs=pl.BlockSpec(memory_space=pltpu.VMEM),
        scratch_shapes=[
            pltpu.VMEM((4 * CH, (PLANE + 1) * SPAN), BF16),
            pltpu.VMEM((SPAN, 256), BF16),
            pltpu.VMEM((256, CHUNK + 128), F32),
            pltpu.VMEM((24, SPAN), F32),
        ],
        name="correlate",
    )(info, record, follower, templates)


def combine_kernel(part_ref, score_ref, arrived, quad, s_xy, r_xy, s_q, r_q):
    me = {a: lax.axis_index(a) for a in AXES}
    greet(me, [("y", "x"), ("zl", "core")])
    here = spot(me, ("y", "x"))
    flat = steps(("y", "x"))
    out = []
    for by in flat:
        to = moved(me, by)
        there = spot(to, ("y", "x"))
        copy = remote(part_ref.at[there], arrived.at[here], s_xy.at[there], r_xy.at[here], to)
        copy.start()
        out.append(copy)
    arrived[here] = part_ref[here]
    for by in flat:
        source = moved(me, by, -1)
        there = spot(source, ("y", "x"))
        remote(part_ref.at[there], arrived.at[there], s_xy.at[there], r_xy.at[there], source).wait_recv()
    mine = spot(me, ("zl", "core"))
    quad[mine] = jnp.sum(arrived[...], axis=0)
    near = steps(("zl", "core"))
    for by in near:
        to = moved(me, by)
        copy = remote(quad.at[mine], quad.at[mine], s_q.at[spot(to, ("zl", "core"))], r_q.at[mine], to)
        copy.start()
        out.append(copy)
    for by in near:
        source = moved(me, by, -1)
        there = spot(source, ("zl", "core"))
        remote(quad.at[there], quad.at[there], s_q.at[there], r_q.at[there], source).wait_recv()
    total = (quad[0] + quad[1]) + (quad[2] + quad[3])
    corner = total[:, SPAN:WIDE]
    energy = jnp.concatenate([corner[i : i + 1, :] for i in range(4)], axis=1)
    row = lax.broadcasted_iota(jnp.int32, (EVENTS, 128), 0)
    col = lax.broadcasted_iota(jnp.int32, (EVENTS, 128), 1)
    norm = jnp.sum(jnp.where(row == col, corner[4:5, :], 0.0), axis=1, keepdims=True)
    score_ref[...] = total[:, 0:SPAN] / jnp.sqrt(energy * norm + 1e-6)
    for copy in out:
        copy.wait_send()


def combine(parts):
    dma = pltpu.SemaphoreType.DMA
    return pl.pallas_call(
        combine_kernel,
        out_shape=jax.ShapeDtypeStruct((EVENTS, SPAN), F32),
        in_specs=[pl.BlockSpec(memory_space=pltpu.VMEM)],
        out_specs=pl.BlockSpec(memory_space=pltpu.VMEM),
        scratch_shapes=[
            pltpu.VMEM((PLANE, EVENTS, WIDE), F32),
            pltpu.VMEM((4, EVENTS, WIDE), F32),
            dma((PLANE,)),
            dma((PLANE,)),
            dma((4,)),
            dma((4,)),
        ],
        compiler_params=pltpu.CompilerParams(collective_id=1, has_side_effects=True),
        name="combine",
    )(parts)


def local(record, event_stretch, event_offset):
    where = event_stretch.reshape(EVENTS)
    plane = lax.axis_index("zh").astype(jnp.int32)
    info = jnp.concatenate([event_offset.reshape(EVENTS), plane[None]])
    taken, follower, templates = exchange(where, record)
    parts = correlate(info, taken, follower, templates)
    return combine(parts).reshape(4, 2, SPAN)


def solution(mesh):
    torus = Mesh(mesh.devices.reshape(4, 4, 4, 2, 2), AXES)
    return jax.shard_map(
        local,
        mesh=torus,
        in_specs=(P(("zl", "core"), ("zh", "y", "x")), P(), P()),
        out_specs=P(None, None, ("zh", "y", "x")),
        check_vma=False,
    )
```

```python
import functools
import itertools

import jax
import jax.numpy as jnp
from jax import lax
from jax.experimental import pallas as pl
from jax.experimental.pallas import tpu as pltpu
from jax.sharding import Mesh
from jax.sharding import PartitionSpec as P

TAPS = 500
AXES = ("zh", "y", "x", "zl", "core")
SIZE = {"zh": 4, "y": 4, "x": 4, "zl": 2, "core": 2}
MESH = pl.DeviceIdType.MESH
F32 = jnp.float32
BF16 = jnp.bfloat16
SPAN = 512
PLANE = 16
CH = 32
HALF = 16
EVENTS = 8
SUB = 32
CHUNK = 2048
WIDE = SPAN + 128


def steps(axes):
    grid = itertools.product(*[range(SIZE[a]) for a in axes])
    return [dict(zip(axes, at)) for at in grid if any(at)]


def moved(me, by, sign=1):
    return {a: lax.rem(me[a] + sign * by[a] + SIZE[a], SIZE[a]) for a in by}


def spot(at, axes):
    index = 0
    for a in axes:
        index = index * SIZE[a] + at[a]
    return index


def remote(src, dst, send, recv, to):
    return pltpu.make_async_remote_copy(
        src_ref=src, dst_ref=dst, send_sem=send, recv_sem=recv, device_id=to, device_id_type=MESH
    )


def greet(me, groups):
    barrier = pltpu.get_barrier_semaphore()
    count = 0
    for axes in groups:
        for by in steps(axes):
            pl.semaphore_signal(barrier, inc=1, device_id=moved(me, by), device_id_type=MESH)
            count += 1
    pl.semaphore_wait(barrier, count)


def left(x, by):
    return pltpu.roll(x, x.shape[1] - by, 1) if by else x


def kernel(
    stretch_ref,
    offset_ref,
    x_ref,
    score_ref,
    rec0,
    rec1,
    next0,
    next1,
    cand0,
    cand1,
    picks0,
    picks1,
    tmpl0,
    tmpl1,
    phases,
    taps,
    product0,
    product1,
    power,
    part,
    arrived,
    quad,
    s_xy,
    r_xy,
    s_z,
    r_z,
    s_g,
    r_g,
    s_h,
    r_h,
    own,
    s_p,
    r_p,
    s_q,
    r_q,
):
    me = {a: lax.axis_index(a) for a in AXES}
    greet(me, [("y", "x"), ("zh",), ("zl", "core")])
    here = spot(me, ("y", "x"))
    zh = me["zh"]
    flat = steps(("y", "x"))
    recs, nexts, cands, pickss, tmpls = (rec0, rec1), (next0, next1), (cand0, cand1), (picks0, picks1), (tmpl0, tmpl1)
    out = []

    kept = []
    for h in range(2):
        rows = slice(HALF * h, HALF * h + HALF)
        for by in flat:
            to = moved(me, by)
            there = spot(to, ("y", "x"))
            copy = remote(
                x_ref.at[there, rows], recs[h].at[here], s_xy.at[h, there], r_xy.at[h, here], to
            )
            copy.start()
            out.append(copy)
        keep = pltpu.make_async_copy(x_ref.at[here, rows], recs[h].at[here], own.at[h])
        keep.start()
        kept.append(keep)

    back = {"zh": lax.rem(zh + 3, 4)}
    halos = []
    for h in range(2):
        rows = slice(HALF * h, HALF * h + HALF)
        kept[h].wait()
        for by in flat:
            source = moved(me, by, -1)
            there = spot(source, ("y", "x"))
            remote(
                x_ref.at[there, rows], recs[h].at[there], s_xy.at[h, there], r_xy.at[h, there], source
            ).wait_recv()
        for j in range(EVENTS):
            cands[h][j // 2, j % 2] = recs[h][lax.rem(stretch_ref[j // 2, j % 2], PLANE)]
        for d in (2, 1, 3):
            q = lax.rem(zh + d, 4)
            copy = remote(cands[h].at[q], pickss[h].at[zh], s_z.at[h, q], r_z.at[h, zh], {"zh": q})
            copy.start()
            out.append(copy)
        pickss[h][zh] = cands[h][zh]
    for h in range(2):
        halo = remote(recs[h].at[0], nexts[h], s_h.at[h], r_h.at[h], back)
        halo.start()
        halos.append(halo)

    tap = lax.broadcasted_iota(jnp.int32, (HALF, SPAN), 1)
    for h in range(2):
        for d in (1, 2, 3):
            q = lax.rem(zh + d, 4)
            remote(cands[h].at[q], pickss[h].at[q], s_z.at[h, q], r_z.at[h, q], {"zh": q}).wait_recv()
        for i in range(2):
            wide = pickss[h][lax.div(stretch_ref[zh, i], PLANE), i].astype(F32)
            shift = jnp.full((HALF, SPAN), offset_ref[zh, i], jnp.int32)
            for bit in (1, 2, 4, 8):
                wide = jnp.where((shift & bit) != 0, left(wide, bit), wide)
            tmpls[h][zh, i] = jnp.where(tap < TAPS, wide, 0.0).astype(BF16)
        for d in (2, 1, 3):
            q = lax.rem(zh + d, 4)
            copy = remote(tmpls[h].at[zh], tmpls[h].at[zh], s_g.at[h, q], r_g.at[h, zh], {"zh": q})
            copy.start()
            out.append(copy)

    def fill(s, here, after):
        total = None
        at = pl.multiple_of(s * SPAN, SPAN)
        for h in range(2):
            wide = here[h].astype(F32)
            square = jnp.sum(wide * wide, axis=0, keepdims=True)
            total = square if h == 0 else total + square
            joined = jnp.concatenate([here[h], after[h]], axis=1)
            for p in range(4):
                row = p * CH + h * HALF
                phases[row : row + HALF, pl.ds(at, SPAN)] = left(joined, SUB * p)[:, :SPAN]
        power[pl.ds(s, 1), :] = total

    @pl.loop(0, PLANE - 1)
    def _(s):
        fill(s, [r[s] for r in recs], [r[s + 1, :, 0:128] for r in recs])

    for halo in halos:
        halo.wait_recv()
    inside = (zh < 3).astype(F32)
    follow = [(n[...].astype(F32) * inside).astype(BF16) for n in nexts]
    fill(PLANE - 1, [r[PLANE - 1] for r in recs], [f[:, 0:128] for f in follow])
    fill(PLANE, follow, [jnp.zeros((HALF, 128), BF16)] * 2)

    double = jnp.concatenate([power[0:PLANE, :], power[1 : PLANE + 1, :]], axis=1)
    sums = {1: double}
    for size in (1, 2, 4, 8, 16, 32, 64, 128):
        sums[2 * size] = sums[size] + left(sums[size], size)
    energy = sums[256][:, :SPAN]
    start = 256
    for size in (128, 64, 32, 16, 4):
        energy = energy + left(sums[size], start)[:, :SPAN]
        start += size
    for s in range(PLANE):
        for i in range(4):
            part[s, i : i + 1, SPAN:WIDE] = energy[s : s + 1, 128 * i : 128 * i + 128]

    row = lax.broadcasted_iota(jnp.int32, (256, 256), 0)
    col = lax.broadcasted_iota(jnp.int32, (256, 256), 1)
    order = (lax.rem(row, 8) * SUB + lax.div(row, 8) == col).astype(F32).astype(BF16)
    group = lax.div(lax.broadcasted_iota(jnp.int32, (HALF, 128), 1), SUB).astype(F32).astype(BF16)
    for h in range(2):
        for d in (1, 2, 3):
            q = lax.rem(zh + d, 4)
            remote(tmpls[h].at[q], tmpls[h].at[q], s_g.at[h, q], r_g.at[h, q], {"zh": q}).wait_recv()
        for half in range(2):
            for m in range(4):
                pieces = [
                    tmpls[h][(4 * half + i) // 2, i % 2, :, 128 * m : 128 * m + 128] for i in range(4)
                ]
                for p in range(4):
                    tile = left(pieces[0], SUB * p)
                    for i in range(1, 4):
                        tile = jnp.where(group == i, left(pieces[i], SUB * (p - i) % 128), tile)
                    at = (4 * m + p) * CH + HALF * h
                    taps[at : at + HALF, 128 * half : 128 * half + 128] = tile
    weights = lax.dot_general(
        order, taps[...], (((1,), (1,)), ((), ())), preferred_element_type=F32
    ).astype(BF16)

    spread = lax.broadcasted_iota(jnp.int32, (1, 128), 1)
    norms = jnp.zeros((1, 128), F32)
    for j in range(EVENTS):
        both = [t[j // 2, j % 2].astype(F32) for t in tmpls]
        norm = jnp.sum(both[0] * both[0] + both[1] * both[1], keepdims=True)
        norms = jnp.where(spread == j, norm, norms)
    rest = jnp.concatenate([norms, jnp.zeros((3, 128), F32)], axis=0)
    for s in range(PLANE):
        part[s, 4:8, SPAN:WIDE] = rest

    products = (product0, product1)
    turns = [lax.rem(me["y"] + d, 4) for d in (2, 1, 3, 0)]

    def multiply(i):
        at = pl.multiple_of(turns[i] * CHUNK, CHUNK)
        stack = jnp.concatenate([phases[:, pl.ds(at + 128 * m, CHUNK + 128)] for m in range(4)], axis=0)
        products[i % 2][...] = jnp.dot(weights, stack, preferred_element_type=F32)

    multiply(0)
    for i in range(4):
        if i < 3:
            multiply(i + 1)
        product = products[i % 2]
        total = product[0:8, 0:CHUNK]
        for b in range(1, SUB):
            total = total + left(product[8 * b : 8 * b + 8, :], b)[:, :CHUNK]
        for q in range(4):
            part[turns[i] * 4 + q, :, 0:SPAN] = total[:, SPAN * q : SPAN * q + SPAN]
        for dx in (2, 1, 3, 0):
            if i == 3 and dx == 0:
                continue
            to = {"y": turns[i], "x": lax.rem(me["x"] + dx, 4)}
            there = spot(to, ("y", "x"))
            copy = remote(part.at[there], arrived.at[here], s_p.at[there], r_p.at[here], to)
            copy.start()
            out.append(copy)
    arrived[here] = part[here]
    for by in flat:
        source = moved(me, by, -1)
        there = spot(source, ("y", "x"))
        remote(part.at[there], arrived.at[there], s_p.at[there], r_p.at[there], source).wait_recv()

    mine = spot(me, ("zl", "core"))
    quad[mine] = jnp.sum(arrived[...], axis=0)
    near = steps(("zl", "core"))
    for by in near[::-1]:
        to = moved(me, by)
        copy = remote(quad.at[mine], quad.at[mine], s_q.at[spot(to, ("zl", "core"))], r_q.at[mine], to)
        copy.start()
        out.append(copy)
    for by in near:
        source = moved(me, by, -1)
        there = spot(source, ("zl", "core"))
        remote(quad.at[there], quad.at[there], s_q.at[there], r_q.at[there], source).wait_recv()
    total = (quad[0] + quad[1]) + (quad[2] + quad[3])
    corner = total[:, SPAN:WIDE]
    energy = jnp.concatenate([corner[i : i + 1, :] for i in range(4)], axis=1)
    row = lax.broadcasted_iota(jnp.int32, (EVENTS, 128), 0)
    col = lax.broadcasted_iota(jnp.int32, (EVENTS, 128), 1)
    norm = jnp.sum(jnp.where(row == col, corner[4:5, :], 0.0), axis=1, keepdims=True)
    score = total[:, 0:SPAN] / jnp.sqrt(energy * norm + 1e-6)
    for i in range(4):
        score_ref[i] = score[2 * i : 2 * i + 2, :]
    for copy in out:
        copy.wait_send()
    for halo in halos:
        halo.wait_send()


def local(record, event_stretch, event_offset):
    dma = pltpu.SemaphoreType.DMA
    blocks = pltpu.VMEM((PLANE, HALF, SPAN), BF16)
    pairs = pltpu.VMEM((4, 2, HALF, SPAN), BF16)
    return pl.pallas_call(
        kernel,
        out_shape=jax.ShapeDtypeStruct((4, 2, SPAN), F32),
        in_specs=[pl.BlockSpec(memory_space=pltpu.SMEM)] * 2 + [pl.BlockSpec(memory_space=pl.ANY)],
        out_specs=pl.BlockSpec(memory_space=pltpu.VMEM),
        scratch_shapes=[blocks] * 2
        + [pltpu.VMEM((HALF, SPAN), BF16)] * 2
        + [pairs] * 6
        + [
            pltpu.VMEM((4 * CH, (PLANE + 1) * SPAN), BF16),
            pltpu.VMEM((SPAN, 256), BF16),
            pltpu.VMEM((256, CHUNK + 128), F32),
            pltpu.VMEM((256, CHUNK + 128), F32),
            pltpu.VMEM((24, SPAN), F32),
            pltpu.VMEM((PLANE, EVENTS, WIDE), F32),
            pltpu.VMEM((PLANE, EVENTS, WIDE), F32),
            pltpu.VMEM((4, EVENTS, WIDE), F32),
        ]
        + [dma((2, PLANE))] * 2
        + [dma((2, 4))] * 4
        + [dma((2,))] * 3
        + [dma((PLANE,))] * 2
        + [dma((4,))] * 2,
        compiler_params=pltpu.CompilerParams(collective_id=0, has_side_effects=True),
        name="matching",
    )(event_stretch, event_offset, record.reshape(PLANE, CH, SPAN))


def solution(mesh):
    torus = Mesh(mesh.devices.reshape(4, 4, 4, 2, 2), AXES)
    return jax.shard_map(
        local,
        mesh=torus,
        in_specs=(P(("zl", "core"), ("zh", "y", "x")), P(), P()),
        out_specs=P(None, None, ("zh", "y", "x")),
        check_vma=False,
    )
```

```python
import functools
import itertools

import jax
import jax.numpy as jnp
from jax import lax
from jax.experimental import pallas as pl
from jax.experimental.pallas import tpu as pltpu
from jax.sharding import Mesh
from jax.sharding import PartitionSpec as P

TAPS = 500
AXES = ("zh", "y", "x", "zl", "core")
SIZE = {"zh": 4, "y": 4, "x": 4, "zl": 2, "core": 2}
MESH = pl.DeviceIdType.MESH
F32 = jnp.float32
BF16 = jnp.bfloat16
SPAN = 512
PLANE = 16
CH = 32
HALF = 16
EVENTS = 8
SUB = 32
CHUNK = 2048


def steps(axes):
    grid = itertools.product(*[range(SIZE[a]) for a in axes])
    return [dict(zip(axes, at)) for at in grid if any(at)]


def moved(me, by, sign=1):
    return {a: lax.rem(me[a] + sign * by[a] + SIZE[a], SIZE[a]) for a in by}


def spot(at, axes):
    index = 0
    for a in axes:
        index = index * SIZE[a] + at[a]
    return index


def remote(src, dst, send, recv, to):
    return pltpu.make_async_remote_copy(
        src_ref=src, dst_ref=dst, send_sem=send, recv_sem=recv, device_id=to, device_id_type=MESH
    )


def greet(me, groups):
    barrier = pltpu.get_barrier_semaphore()
    count = 0
    for axes in groups:
        for by in steps(axes):
            pl.semaphore_signal(barrier, inc=1, device_id=moved(me, by), device_id_type=MESH)
            count += 1
    pl.semaphore_wait(barrier, count)


def left(x, by):
    return pltpu.roll(x, x.shape[1] - by, 1) if by else x


def kernel(
    stretch_ref,
    offset_ref,
    x_ref,
    score_ref,
    rec0,
    rec1,
    next0,
    next1,
    cand0,
    cand1,
    picks0,
    picks1,
    tmpl0,
    tmpl1,
    phases,
    taps,
    product0,
    product1,
    power,
    part,
    arrived,
    quad,
    side,
    sides,
    corner,
    s_xy,
    r_xy,
    s_z,
    r_z,
    s_g,
    r_g,
    s_h,
    r_h,
    own,
    s_p,
    r_p,
    s_q,
    r_q,
    s_e,
    r_e,
    s_c,
    r_c,
):
    me = {a: lax.axis_index(a) for a in AXES}
    greet(me, [("y", "x"), ("zh",), ("zl", "core")])
    here = spot(me, ("y", "x"))
    zh = me["zh"]
    flat = steps(("y", "x"))
    recs, nexts, cands, pickss, tmpls = (rec0, rec1), (next0, next1), (cand0, cand1), (picks0, picks1), (tmpl0, tmpl1)
    out = []

    kept = []
    for h in range(2):
        rows = slice(HALF * h, HALF * h + HALF)
        for by in flat:
            to = moved(me, by)
            there = spot(to, ("y", "x"))
            copy = remote(
                x_ref.at[there, rows], recs[h].at[here], s_xy.at[h, there], r_xy.at[h, here], to
            )
            copy.start()
            out.append(copy)
        keep = pltpu.make_async_copy(x_ref.at[here, rows], recs[h].at[here], own.at[h])
        keep.start()
        kept.append(keep)

    back = {"zh": lax.rem(zh + 3, 4)}
    halos = []
    for h in range(2):
        rows = slice(HALF * h, HALF * h + HALF)
        kept[h].wait()
        for by in flat:
            source = moved(me, by, -1)
            there = spot(source, ("y", "x"))
            remote(
                x_ref.at[there, rows], recs[h].at[there], s_xy.at[h, there], r_xy.at[h, there], source
            ).wait_recv()
        for j in range(EVENTS):
            cands[h][j // 2, j % 2] = recs[h][lax.rem(stretch_ref[j % 2, j // 2], PLANE)]
        for d in (2, 1, 3):
            q = lax.rem(zh + d, 4)
            copy = remote(cands[h].at[q], pickss[h].at[zh], s_z.at[h, q], r_z.at[h, zh], {"zh": q})
            copy.start()
            out.append(copy)
        pickss[h][zh] = cands[h][zh]
    for h in range(2):
        halo = remote(recs[h].at[0], nexts[h], s_h.at[h], r_h.at[h], back)
        halo.start()
        halos.append(halo)

    tap = lax.broadcasted_iota(jnp.int32, (HALF, SPAN), 1)
    for h in range(2):
        for d in (1, 2, 3):
            q = lax.rem(zh + d, 4)
            remote(cands[h].at[q], pickss[h].at[q], s_z.at[h, q], r_z.at[h, q], {"zh": q}).wait_recv()
        for i in range(2):
            wide = pickss[h][lax.div(stretch_ref[i, zh], PLANE), i].astype(F32)
            shift = jnp.full((HALF, SPAN), offset_ref[i, zh], jnp.int32)
            for bit in (1, 2, 4, 8):
                wide = jnp.where((shift & bit) != 0, left(wide, bit), wide)
            tmpls[h][zh, i] = jnp.where(tap < TAPS, wide, 0.0).astype(BF16)
        for d in (2, 1, 3):
            q = lax.rem(zh + d, 4)
            copy = remote(tmpls[h].at[zh], tmpls[h].at[zh], s_g.at[h, q], r_g.at[h, zh], {"zh": q})
            copy.start()
            out.append(copy)

    def fill(s, here, after):
        total = None
        at = pl.multiple_of(s * SPAN, SPAN)
        for h in range(2):
            wide = here[h].astype(F32)
            square = jnp.sum(wide * wide, axis=0, keepdims=True)
            total = square if h == 0 else total + square
            joined = jnp.concatenate([here[h], after[h]], axis=1)
            for p in range(4):
                row = p * CH + h * HALF
                phases[row : row + HALF, pl.ds(at, SPAN)] = left(joined, SUB * p)[:, :SPAN]
        power[pl.ds(s, 1), :] = total

    @pl.loop(0, PLANE - 1)
    def _(s):
        fill(s, [r[s] for r in recs], [r[s + 1, :, 0:128] for r in recs])

    for halo in halos:
        halo.wait_recv()
    inside = (zh < 3).astype(F32)
    follow = [(n[...].astype(F32) * inside).astype(BF16) for n in nexts]
    fill(PLANE - 1, [r[PLANE - 1] for r in recs], [f[:, 0:128] for f in follow])
    fill(PLANE, follow, [jnp.zeros((HALF, 128), BF16)] * 2)

    double = jnp.concatenate([power[0:PLANE, :], power[1 : PLANE + 1, :]], axis=1)
    sums = {1: double}
    for size in (1, 2, 4, 8, 16, 32, 64, 128):
        sums[2 * size] = sums[size] + left(sums[size], size)
    energy = sums[256][:, :SPAN]
    start = 256
    for size in (128, 64, 32, 16, 4):
        energy = energy + left(sums[size], start)[:, :SPAN]
        start += size
    for s in range(PLANE):
        for i in range(4):
            side[s, i : i + 1, :] = energy[s : s + 1, 128 * i : 128 * i + 128]

    row = lax.broadcasted_iota(jnp.int32, (256, 256), 0)
    col = lax.broadcasted_iota(jnp.int32, (256, 256), 1)
    order = (lax.rem(row, 8) * SUB + lax.div(row, 8) == col).astype(F32).astype(BF16)
    group = lax.div(lax.broadcasted_iota(jnp.int32, (HALF, 128), 1), SUB).astype(F32).astype(BF16)
    for h in range(2):
        for d in (1, 2, 3):
            q = lax.rem(zh + d, 4)
            remote(tmpls[h].at[q], tmpls[h].at[q], s_g.at[h, q], r_g.at[h, q], {"zh": q}).wait_recv()
        for half in range(2):
            for m in range(4):
                pieces = [
                    tmpls[h][(4 * half + i) // 2, i % 2, :, 128 * m : 128 * m + 128] for i in range(4)
                ]
                for p in range(4):
                    tile = left(pieces[0], SUB * p)
                    for i in range(1, 4):
                        tile = jnp.where(group == i, left(pieces[i], SUB * (p - i) % 128), tile)
                    at = (4 * m + p) * CH + HALF * h
                    taps[at : at + HALF, 128 * half : 128 * half + 128] = tile
    weights = lax.dot_general(
        order, taps[...], (((1,), (1,)), ((), ())), preferred_element_type=F32
    ).astype(BF16)

    spread = lax.broadcasted_iota(jnp.int32, (1, 128), 1)
    norms = jnp.zeros((1, 128), F32)
    for j in range(EVENTS):
        both = [t[j // 2, j % 2].astype(F32) for t in tmpls]
        norm = jnp.sum(both[0] * both[0] + both[1] * both[1], keepdims=True)
        norms = jnp.where(spread == j, norm, norms)
    rest = jnp.concatenate([norms, jnp.zeros((3, 128), F32)], axis=0)
    for s in range(PLANE):
        side[s, 4:8, :] = rest
    for by in flat:
        to = moved(me, by)
        there = spot(to, ("y", "x"))
        copy = remote(side.at[there], sides.at[here], s_e.at[there], r_e.at[here], to)
        copy.start()
        out.append(copy)
    sides[here] = side[here]
    near = steps(("zl", "core"))
    mine = spot(me, ("zl", "core"))

    products = (product0, product1)
    turns = [lax.rem(me["y"] + d, 4) for d in (2, 1, 3, 0)]

    def multiply(i):
        at = pl.multiple_of(turns[i] * CHUNK, CHUNK)
        stack = jnp.concatenate([phases[:, pl.ds(at + 128 * m, CHUNK + 128)] for m in range(4)], axis=0)
        products[i % 2][...] = jnp.dot(weights, stack, preferred_element_type=F32)

    multiply(0)
    for i in range(4):
        if i < 3:
            multiply(i + 1)
        product = products[i % 2]
        total = product[0:8, 0:CHUNK]
        for b in range(1, SUB):
            total = total + left(product[8 * b : 8 * b + 8, :], b)[:, :CHUNK]
        for q in range(4):
            part[turns[i] * 4 + q] = total[:, SPAN * q : SPAN * q + SPAN]
        for dx in (2, 1, 3, 0):
            if i == 3 and dx == 0:
                continue
            to = {"y": turns[i], "x": lax.rem(me["x"] + dx, 4)}
            there = spot(to, ("y", "x"))
            copy = remote(part.at[there], arrived.at[here], s_p.at[there], r_p.at[here], to)
            copy.start()
            out.append(copy)
        if i == 2:
            for by in flat:
                source = moved(me, by, -1)
                there = spot(source, ("y", "x"))
                remote(side.at[there], sides.at[there], s_e.at[there], r_e.at[there], source).wait_recv()
            corner[mine] = jnp.sum(sides[...], axis=0)
            for by in near:
                to = moved(me, by)
                there = spot(to, ("zl", "core"))
                copy = remote(corner.at[mine], corner.at[mine], s_c.at[there], r_c.at[mine], to)
                copy.start()
                out.append(copy)
    for by in near:
        source = moved(me, by, -1)
        there = spot(source, ("zl", "core"))
        remote(corner.at[there], corner.at[there], s_c.at[there], r_c.at[there], source).wait_recv()
    ends = (corner[0] + corner[1]) + (corner[2] + corner[3])
    energy = jnp.concatenate([ends[i : i + 1, :] for i in range(4)], axis=1)
    row = lax.broadcasted_iota(jnp.int32, (EVENTS, 128), 0)
    col = lax.broadcasted_iota(jnp.int32, (EVENTS, 128), 1)
    norm = jnp.sum(jnp.where(row == col, ends[4:5, :], 0.0), axis=1, keepdims=True)
    root = jnp.sqrt(energy * norm + 1e-6)
    arrived[here] = part[here]
    for by in flat:
        source = moved(me, by, -1)
        there = spot(source, ("y", "x"))
        remote(part.at[there], arrived.at[there], s_p.at[there], r_p.at[there], source).wait_recv()

    quad[mine] = jnp.sum(arrived[...], axis=0)
    for by in near[::-1]:
        to = moved(me, by)
        copy = remote(quad.at[mine], quad.at[mine], s_q.at[spot(to, ("zl", "core"))], r_q.at[mine], to)
        copy.start()
        out.append(copy)
    for by in near:
        source = moved(me, by, -1)
        there = spot(source, ("zl", "core"))
        remote(quad.at[there], quad.at[there], s_q.at[there], r_q.at[there], source).wait_recv()
    total = (quad[0] + quad[1]) + (quad[2] + quad[3])
    score = total / root
    for i in range(4):
        score_ref[i] = score[2 * i : 2 * i + 2, :]
    for copy in out:
        copy.wait_send()
    for halo in halos:
        halo.wait_send()


def local(record, event_stretch, event_offset):
    dma = pltpu.SemaphoreType.DMA
    blocks = pltpu.VMEM((PLANE, HALF, SPAN), BF16)
    pairs = pltpu.VMEM((4, 2, HALF, SPAN), BF16)
    return pl.pallas_call(
        kernel,
        out_shape=jax.ShapeDtypeStruct((4, 2, SPAN), F32),
        in_specs=[pl.BlockSpec(memory_space=pltpu.SMEM)] * 2 + [pl.BlockSpec(memory_space=pl.ANY)],
        out_specs=pl.BlockSpec(memory_space=pltpu.VMEM),
        scratch_shapes=[blocks] * 2
        + [pltpu.VMEM((HALF, SPAN), BF16)] * 2
        + [pairs] * 6
        + [
            pltpu.VMEM((4 * CH, (PLANE + 1) * SPAN), BF16),
            pltpu.VMEM((SPAN, 256), BF16),
            pltpu.VMEM((256, CHUNK + 128), F32),
            pltpu.VMEM((256, CHUNK + 128), F32),
            pltpu.VMEM((24, SPAN), F32),
            pltpu.VMEM((PLANE, EVENTS, SPAN), F32),
            pltpu.VMEM((PLANE, EVENTS, SPAN), F32),
            pltpu.VMEM((4, EVENTS, SPAN), F32),
            pltpu.VMEM((PLANE, EVENTS, 128), F32),
            pltpu.VMEM((PLANE, EVENTS, 128), F32),
            pltpu.VMEM((4, EVENTS, 128), F32),
        ]
        + [dma((2, PLANE))] * 2
        + [dma((2, 4))] * 4
        + [dma((2,))] * 3
        + [dma((PLANE,)), dma((PLANE,)), dma((4,)), dma((4,))] * 2,
        compiler_params=pltpu.CompilerParams(collective_id=0, has_side_effects=True),
        name="matching",
    )(event_stretch.T, event_offset.T, record.reshape(PLANE, CH, SPAN))


def solution(mesh):
    torus = Mesh(mesh.devices.reshape(4, 4, 4, 2, 2), AXES)
    return jax.shard_map(
        local,
        mesh=torus,
        in_specs=(P(("zl", "core"), ("zh", "y", "x")), P(), P()),
        out_specs=P(None, None, ("zh", "y", "x")),
        check_vma=False,
    )
```

```python
import functools
import itertools

import jax
import jax.numpy as jnp
from jax import lax
from jax.experimental import pallas as pl
from jax.experimental.pallas import tpu as pltpu
from jax.sharding import Mesh
from jax.sharding import PartitionSpec as P

TAPS = 500
AXES = ("zh", "y", "x", "zl", "core")
SIZE = {"zh": 4, "y": 4, "x": 4, "zl": 2, "core": 2}
MESH = pl.DeviceIdType.MESH
F32 = jnp.float32
BF16 = jnp.bfloat16
SPAN = 512
PLANE = 16
CH = 32
PIECES = 4
ROWS = CH // PIECES
EVENTS = 8
SUB = 32
CHUNK = 2048


def steps(axes):
    grid = itertools.product(*[range(SIZE[a]) for a in axes])
    return [dict(zip(axes, at)) for at in grid if any(at)]


def moved(me, by, sign=1):
    return {a: lax.rem(me[a] + sign * by[a] + SIZE[a], SIZE[a]) for a in by}


def spot(at, axes):
    index = 0
    for a in axes:
        index = index * SIZE[a] + at[a]
    return index


def remote(src, dst, send, recv, to):
    return pltpu.make_async_remote_copy(
        src_ref=src, dst_ref=dst, send_sem=send, recv_sem=recv, device_id=to, device_id_type=MESH
    )


def greet(me, groups):
    barrier = pltpu.get_barrier_semaphore()
    count = 0
    for axes in groups:
        for by in steps(axes):
            pl.semaphore_signal(barrier, inc=1, device_id=moved(me, by), device_id_type=MESH)
            count += 1
    pl.semaphore_wait(barrier, count)


def left(x, by):
    return pltpu.roll(x, x.shape[1] - by, 1) if by else x


def settle(ref, count, send, recv, to):
    whole = remote(ref.at[pl.ds(0, count)], ref.at[pl.ds(0, count)], send, recv, to)
    return whole


def kernel(
    stretch_ref,
    offset_ref,
    x_ref,
    score_ref,
    *scratch,
):
    recs, nexts, cands, pickss, tmpls = (scratch[i * PIECES : i * PIECES + PIECES] for i in range(5))
    (
        phases,
        taps,
        product0,
        product1,
        power,
        part,
        arrived,
        quad,
        side,
        sides,
        corner,
        s_xy,
        r_xy,
        s_z,
        r_z,
        s_g,
        r_g,
        s_h,
        r_h,
        own,
        s_p,
        r_p,
        s_q,
        r_q,
        s_e,
        r_e,
        s_c,
        r_c,
    ) = scratch[5 * PIECES :]
    me = {a: lax.axis_index(a) for a in AXES}
    greet(me, [("y", "x"), ("zh",), ("zl", "core")])
    here = spot(me, ("y", "x"))
    zh = me["zh"]
    flat = steps(("y", "x"))
    beside = moved(me, flat[0])
    above = {"zh": lax.rem(zh + 1, 4)}

    kept = []
    for h in range(PIECES):
        rows = slice(ROWS * h, ROWS * h + ROWS)
        for by in flat:
            to = moved(me, by)
            there = spot(to, ("y", "x"))
            remote(x_ref.at[there, rows], recs[h].at[here], s_xy.at[h], r_xy.at[h], to).start()
        keep = pltpu.make_async_copy(x_ref.at[here, rows], recs[h].at[here], own.at[h])
        keep.start()
        kept.append(keep)

    def pick(h):
        settle(pickss[h], 3, s_z.at[h], r_z.at[h], above).wait_recv()
        for i in range(2):
            wide = pickss[h][lax.div(stretch_ref[i, zh], PLANE), i].astype(F32)
            shift = jnp.full((ROWS, SPAN), offset_ref[i, zh], jnp.int32)
            for bit in (1, 2, 4, 8):
                wide = jnp.where((shift & bit) != 0, left(wide, bit), wide)
            tmpls[h][zh, i] = jnp.where(tap < TAPS, wide, 0.0).astype(BF16)
        for d in (2, 1, 3):
            q = lax.rem(zh + d, 4)
            remote(tmpls[h].at[zh], tmpls[h].at[zh], s_g.at[h], r_g.at[h], {"zh": q}).start()

    back = {"zh": lax.rem(zh + 3, 4)}
    tap = lax.broadcasted_iota(jnp.int32, (ROWS, SPAN), 1)
    halos = []
    for h in range(PIECES):
        rows = slice(ROWS * h, ROWS * h + ROWS)
        kept[h].wait()
        settle(recs[h], PLANE - 1, s_xy.at[h], r_xy.at[h], beside).wait_recv()
        for j in range(EVENTS):
            cands[h][j // 2, j % 2] = recs[h][lax.rem(stretch_ref[j % 2, j // 2], PLANE)]
        for d in (2, 1, 3):
            q = lax.rem(zh + d, 4)
            remote(cands[h].at[q], pickss[h].at[zh], s_z.at[h], r_z.at[h], {"zh": q}).start()
        pickss[h][zh] = cands[h][zh]
        if h >= 2:
            pick(h - 2)
    for h in range(PIECES - 2, PIECES):
        pick(h)
    for h in range(PIECES):
        halo = remote(recs[h].at[0], nexts[h], s_h.at[h], r_h.at[h], back)
        halo.start()
        halos.append(halo)

    def merged(blocks):
        if PIECES == 2:
            return blocks
        return [jnp.concatenate(blocks[i : i + 2], axis=0) for i in (0, 2)]

    def fill(s, here, after):
        total = None
        at = pl.multiple_of(s * SPAN, SPAN)
        here, after = merged(here), merged(after)
        for h in range(2):
            wide = here[h].astype(F32)
            square = jnp.sum(wide * wide, axis=0, keepdims=True)
            total = square if h == 0 else total + square
            joined = jnp.concatenate([here[h], after[h]], axis=1)
            for p in range(4):
                row = p * CH + h * 16
                phases[row : row + 16, pl.ds(at, SPAN)] = left(joined, SUB * p)[:, :SPAN]
        power[pl.ds(s, 1), :] = total

    @pl.loop(0, PLANE - 1)
    def _(s):
        fill(s, [r[s] for r in recs], [r[s + 1, :, 0:128] for r in recs])

    for halo in halos:
        halo.wait_recv()
    inside = (zh < 3).astype(F32)
    follow = [(n[...].astype(F32) * inside).astype(BF16) for n in nexts]
    fill(PLANE - 1, [r[PLANE - 1] for r in recs], [f[:, 0:128] for f in follow])
    fill(PLANE, follow, [jnp.zeros((ROWS, 128), BF16)] * PIECES)
    for h in range(PIECES):
        settle(recs[h], PLANE - 1, s_xy.at[h], r_xy.at[h], beside).wait_send()
        settle(pickss[h], 3, s_z.at[h], r_z.at[h], above).wait_send()

    double = jnp.concatenate([power[0:PLANE, :], power[1 : PLANE + 1, :]], axis=1)
    sums = {1: double}
    for size in (1, 2, 4, 8, 16, 32, 64, 128):
        sums[2 * size] = sums[size] + left(sums[size], size)
    energy = sums[256][:, :SPAN]
    start = 256
    for size in (128, 64, 32, 16, 4):
        energy = energy + left(sums[size], start)[:, :SPAN]
        start += size
    for s in range(PLANE):
        for i in range(4):
            side[s, i : i + 1, :] = energy[s : s + 1, 128 * i : 128 * i + 128]

    row = lax.broadcasted_iota(jnp.int32, (256, 256), 0)
    col = lax.broadcasted_iota(jnp.int32, (256, 256), 1)
    order = (lax.rem(row, 8) * SUB + lax.div(row, 8) == col).astype(F32).astype(BF16)
    group = lax.div(lax.broadcasted_iota(jnp.int32, (16, 128), 1), SUB).astype(F32).astype(BF16)
    for h in range(PIECES):
        settle(tmpls[h], 3, s_g.at[h], r_g.at[h], above).wait_recv()
    for h in range(2):
        for half in range(2):
            for m in range(4):
                pieces = [
                    merged([t[(4 * half + i) // 2, i % 2, :, 128 * m : 128 * m + 128] for t in tmpls])[h]
                    for i in range(4)
                ]
                for p in range(4):
                    tile = left(pieces[0], SUB * p)
                    for i in range(1, 4):
                        tile = jnp.where(group == i, left(pieces[i], SUB * (p - i) % 128), tile)
                    at = (4 * m + p) * CH + 16 * h
                    taps[at : at + 16, 128 * half : 128 * half + 128] = tile
    weights = lax.dot_general(
        order, taps[...], (((1,), (1,)), ((), ())), preferred_element_type=F32
    ).astype(BF16)

    spread = lax.broadcasted_iota(jnp.int32, (1, 128), 1)
    norms = jnp.zeros((1, 128), F32)
    for j in range(EVENTS):
        both = [t[j // 2, j % 2].astype(F32) for t in tmpls]
        norm = jnp.sum(sum(b * b for b in both), keepdims=True)
        norms = jnp.where(spread == j, norm, norms)
    rest = jnp.concatenate([norms, jnp.zeros((3, 128), F32)], axis=0)
    for s in range(PLANE):
        side[s, 4:8, :] = rest
    for by in flat:
        to = moved(me, by)
        there = spot(to, ("y", "x"))
        remote(side.at[there], sides.at[here], s_e, r_e, to).start()
    sides[here] = side[here]
    near = steps(("zl", "core"))
    mine = spot(me, ("zl", "core"))

    products = (product0, product1)
    turns = [lax.rem(me["y"] + d, 4) for d in (2, 1, 3, 0)]

    def multiply(i):
        at = pl.multiple_of(turns[i] * CHUNK, CHUNK)
        stack = jnp.concatenate([phases[:, pl.ds(at + 128 * m, CHUNK + 128)] for m in range(4)], axis=0)
        products[i % 2][...] = jnp.dot(weights, stack, preferred_element_type=F32)

    multiply(0)
    for i in range(4):
        if i < 3:
            multiply(i + 1)
        product = products[i % 2]
        total = product[0:8, 0:CHUNK]
        for b in range(1, SUB):
            total = total + left(product[8 * b : 8 * b + 8, :], b)[:, :CHUNK]
        for q in range(4):
            part[turns[i] * 4 + q] = total[:, SPAN * q : SPAN * q + SPAN]
        for dx in (2, 1, 3, 0):
            if i == 3 and dx == 0:
                continue
            to = {"y": turns[i], "x": lax.rem(me["x"] + dx, 4)}
            there = spot(to, ("y", "x"))
            remote(part.at[there], arrived.at[here], s_p, r_p, to).start()
    settle(sides, PLANE - 1, s_e, r_e, beside).wait_recv()
    corner[mine] = jnp.sum(sides[...], axis=0)
    for by in near:
        remote(corner.at[mine], corner.at[mine], s_c, r_c, moved(me, by)).start()
    arrived[here] = part[here]
    settle(arrived, PLANE - 1, s_p, r_p, beside).wait_recv()

    quad[mine] = jnp.sum(arrived[...], axis=0)
    for by in near[::-1]:
        remote(quad.at[mine], quad.at[mine], s_q, r_q, moved(me, by)).start()
    partner = moved(me, near[0])
    settle(corner, 3, s_c, r_c, partner).wait_recv()
    ends = (corner[0] + corner[1]) + (corner[2] + corner[3])
    energy = jnp.concatenate([ends[i : i + 1, :] for i in range(4)], axis=1)
    row = lax.broadcasted_iota(jnp.int32, (EVENTS, 128), 0)
    col = lax.broadcasted_iota(jnp.int32, (EVENTS, 128), 1)
    norm = jnp.sum(jnp.where(row == col, ends[4:5, :], 0.0), axis=1, keepdims=True)
    root = jnp.sqrt(energy * norm + 1e-6)
    settle(sides, PLANE - 1, s_e, r_e, beside).wait_send()
    settle(arrived, PLANE - 1, s_p, r_p, beside).wait_send()
    settle(corner, 3, s_c, r_c, partner).wait_send()
    for h in range(PIECES):
        settle(tmpls[h], 3, s_g.at[h], r_g.at[h], above).wait_send()
        halos[h].wait_send()
    settle(quad, 3, s_q, r_q, partner).wait_recv()
    total = (quad[0] + quad[1]) + (quad[2] + quad[3])
    score = total / root
    for i in range(4):
        score_ref[i] = score[2 * i : 2 * i + 2, :]
    settle(quad, 3, s_q, r_q, partner).wait_send()


def local(record, event_stretch, event_offset):
    dma = pltpu.SemaphoreType.DMA
    blocks = pltpu.VMEM((PLANE, ROWS, SPAN), BF16)
    pairs = pltpu.VMEM((4, 2, ROWS, SPAN), BF16)
    return pl.pallas_call(
        kernel,
        out_shape=jax.ShapeDtypeStruct((4, 2, SPAN), F32),
        in_specs=[pl.BlockSpec(memory_space=pltpu.SMEM)] * 2 + [pl.BlockSpec(memory_space=pl.ANY)],
        out_specs=pl.BlockSpec(memory_space=pltpu.VMEM),
        scratch_shapes=[blocks] * PIECES
        + [pltpu.VMEM((ROWS, SPAN), BF16)] * PIECES
        + [pairs] * (3 * PIECES)
        + [
            pltpu.VMEM((4 * CH, (PLANE + 1) * SPAN), BF16),
            pltpu.VMEM((SPAN, 256), BF16),
            pltpu.VMEM((256, CHUNK + 128), F32),
            pltpu.VMEM((256, CHUNK + 128), F32),
            pltpu.VMEM((24, SPAN), F32),
            pltpu.VMEM((PLANE, EVENTS, SPAN), F32),
            pltpu.VMEM((PLANE, EVENTS, SPAN), F32),
            pltpu.VMEM((4, EVENTS, SPAN), F32),
            pltpu.VMEM((PLANE, EVENTS, 128), F32),
            pltpu.VMEM((PLANE, EVENTS, 128), F32),
            pltpu.VMEM((4, EVENTS, 128), F32),
        ]
        + [dma((PIECES,))] * 9
        + [dma] * 8,
        compiler_params=pltpu.CompilerParams(collective_id=0, has_side_effects=True),
        name="matching",
    )(event_stretch.T, event_offset.T, record.reshape(PLANE, CH, SPAN))


def solution(mesh):
    torus = Mesh(mesh.devices.reshape(4, 4, 4, 2, 2), AXES)
    return jax.shard_map(
        local,
        mesh=torus,
        in_specs=(P(("zl", "core"), ("zh", "y", "x")), P(), P()),
        out_specs=P(None, None, ("zh", "y", "x")),
        check_vma=False,
    )
```

```python
import functools
import itertools

import jax
import jax.numpy as jnp
from jax import lax
from jax.experimental import pallas as pl
from jax.experimental.pallas import tpu as pltpu
from jax.sharding import Mesh
from jax.sharding import PartitionSpec as P

TAPS = 500
AXES = ("zh", "y", "x", "zl", "core")
SIZE = {"zh": 4, "y": 4, "x": 4, "zl": 2, "core": 2}
MESH = pl.DeviceIdType.MESH
F32 = jnp.float32
BF16 = jnp.bfloat16
SPAN = 512
PLANE = 16
CH = 32
PIECES = 4
ROWS = CH // PIECES
EVENTS = 8
SUB = 32
CHUNK = 2048


def steps(axes):
    grid = itertools.product(*[range(SIZE[a]) for a in axes])
    return [dict(zip(axes, at)) for at in grid if any(at)]


def moved(me, by, sign=1):
    return {a: lax.rem(me[a] + sign * by[a] + SIZE[a], SIZE[a]) for a in by}


def spot(at, axes):
    index = 0
    for a in axes:
        index = index * SIZE[a] + at[a]
    return index


def remote(src, dst, send, recv, to):
    return pltpu.make_async_remote_copy(
        src_ref=src, dst_ref=dst, send_sem=send, recv_sem=recv, device_id=to, device_id_type=MESH
    )


def greet(me, groups):
    barrier = pltpu.get_barrier_semaphore()
    count = 0
    for axes in groups:
        for by in steps(axes):
            pl.semaphore_signal(barrier, inc=1, device_id=moved(me, by), device_id_type=MESH)
            count += 1
    pl.semaphore_wait(barrier, count)


def left(x, by):
    return pltpu.roll(x, x.shape[1] - by, 1) if by else x


def settle(ref, count, send, recv, to):
    whole = remote(ref.at[pl.ds(0, count)], ref.at[pl.ds(0, count)], send, recv, to)
    return whole


def kernel(
    stretch_hbm,
    offset_hbm,
    x_ref,
    score_ref,
    root_ref,
    *scratch,
):
    recs, nexts, cands, pickss, tmpls = (scratch[i * PIECES : i * PIECES + PIECES] for i in range(5))
    (
        phases,
        taps,
        product0,
        product1,
        power,
        part,
        arrived,
        quad,
        side,
        sides,
        corner,
        s_xy,
        r_xy,
        s_z,
        r_z,
        s_g,
        r_g,
        s_h,
        r_h,
        own,
        s_p,
        r_p,
        s_q,
        r_q,
        s_e,
        r_e,
        s_c,
        r_c,
        stretch_ref,
        offset_ref,
        r_i,
    ) = scratch[5 * PIECES :]
    me = {a: lax.axis_index(a) for a in AXES}
    tables = [
        pltpu.make_async_copy(stretch_hbm, stretch_ref, r_i.at[0]),
        pltpu.make_async_copy(offset_hbm, offset_ref, r_i.at[1]),
    ]
    for table in tables:
        table.start()
    greet(me, [("y", "x"), ("zh",), ("zl", "core")])
    here = spot(me, ("y", "x"))
    zh = me["zh"]
    flat = steps(("y", "x"))
    beside = moved(me, flat[0])
    above = {"zh": lax.rem(zh + 1, 4)}

    kept = []
    for h in range(PIECES):
        rows = slice(ROWS * h, ROWS * h + ROWS)
        for by in flat:
            to = moved(me, by)
            there = spot(to, ("y", "x"))
            remote(x_ref.at[there, rows], recs[h].at[here], s_xy.at[h], r_xy.at[h], to).start()
        keep = pltpu.make_async_copy(x_ref.at[here, rows], recs[h].at[here], own.at[h])
        keep.start()
        kept.append(keep)

    for table in tables:
        table.wait()

    def pick(h):
        settle(pickss[h], 3, s_z.at[h], r_z.at[h], above).wait_recv()
        for i in range(2):
            wide = pickss[h][lax.div(stretch_ref[i, zh], PLANE), i].astype(F32)
            shift = jnp.full((ROWS, SPAN), offset_ref[i, zh], jnp.int32)
            for bit in (1, 2, 4, 8):
                wide = jnp.where((shift & bit) != 0, left(wide, bit), wide)
            tmpls[h][zh, i] = jnp.where(tap < TAPS, wide, 0.0).astype(BF16)
        for d in (2, 1, 3):
            q = lax.rem(zh + d, 4)
            remote(tmpls[h].at[zh], tmpls[h].at[zh], s_g.at[h], r_g.at[h], {"zh": q}).start()

    back = {"zh": lax.rem(zh + 3, 4)}
    tap = lax.broadcasted_iota(jnp.int32, (ROWS, SPAN), 1)
    halos = []
    for h in range(PIECES):
        rows = slice(ROWS * h, ROWS * h + ROWS)
        kept[h].wait()
        settle(recs[h], PLANE - 1, s_xy.at[h], r_xy.at[h], beside).wait_recv()
        for j in range(EVENTS):
            cands[h][j // 2, j % 2] = recs[h][lax.rem(stretch_ref[j % 2, j // 2], PLANE)]
        for d in (2, 1, 3):
            q = lax.rem(zh + d, 4)
            remote(cands[h].at[q], pickss[h].at[zh], s_z.at[h], r_z.at[h], {"zh": q}).start()
        pickss[h][zh] = cands[h][zh]
        if h >= 2:
            pick(h - 2)
    for h in range(PIECES - 2, PIECES):
        pick(h)
    for h in range(PIECES):
        halo = remote(recs[h].at[0], nexts[h], s_h.at[h], r_h.at[h], back)
        halo.start()
        halos.append(halo)

    def merged(blocks):
        if PIECES == 2:
            return blocks
        return [jnp.concatenate(blocks[i : i + 2], axis=0) for i in (0, 2)]

    def fill(s, here, after):
        total = None
        at = pl.multiple_of(s * SPAN, SPAN)
        here, after = merged(here), merged(after)
        for h in range(2):
            wide = here[h].astype(F32)
            square = jnp.sum(wide * wide, axis=0, keepdims=True)
            total = square if h == 0 else total + square
            joined = jnp.concatenate([here[h], after[h]], axis=1)
            for p in range(4):
                row = p * CH + h * 16
                phases[row : row + 16, pl.ds(at, SPAN)] = left(joined, SUB * p)[:, :SPAN]
        power[pl.ds(s, 1), :] = total

    @pl.loop(0, PLANE - 1)
    def _(s):
        fill(s, [r[s] for r in recs], [r[s + 1, :, 0:128] for r in recs])

    for halo in halos:
        halo.wait_recv()
    inside = (zh < 3).astype(F32)
    follow = [(n[...].astype(F32) * inside).astype(BF16) for n in nexts]
    fill(PLANE - 1, [r[PLANE - 1] for r in recs], [f[:, 0:128] for f in follow])
    fill(PLANE, follow, [jnp.zeros((ROWS, 128), BF16)] * PIECES)
    for h in range(PIECES):
        settle(recs[h], PLANE - 1, s_xy.at[h], r_xy.at[h], beside).wait_send()
        settle(pickss[h], 3, s_z.at[h], r_z.at[h], above).wait_send()

    double = jnp.concatenate([power[0:PLANE, :], power[1 : PLANE + 1, :]], axis=1)
    sums = {1: double}
    for size in (1, 2, 4, 8, 16, 32, 64, 128):
        sums[2 * size] = sums[size] + left(sums[size], size)
    energy = sums[256][:, :SPAN]
    start = 256
    for size in (128, 64, 32, 16, 4):
        energy = energy + left(sums[size], start)[:, :SPAN]
        start += size
    for s in range(PLANE):
        for i in range(4):
            side[s, i : i + 1, :] = energy[s : s + 1, 128 * i : 128 * i + 128]

    row = lax.broadcasted_iota(jnp.int32, (256, 256), 0)
    col = lax.broadcasted_iota(jnp.int32, (256, 256), 1)
    order = (lax.rem(row, 8) * SUB + lax.div(row, 8) == col).astype(F32).astype(BF16)
    group = lax.div(lax.broadcasted_iota(jnp.int32, (16, 128), 1), SUB).astype(F32).astype(BF16)
    for h in range(PIECES):
        settle(tmpls[h], 3, s_g.at[h], r_g.at[h], above).wait_recv()
    for h in range(2):
        for half in range(2):
            for m in range(4):
                pieces = [
                    merged([t[(4 * half + i) // 2, i % 2, :, 128 * m : 128 * m + 128] for t in tmpls])[h]
                    for i in range(4)
                ]
                for p in range(4):
                    tile = left(pieces[0], SUB * p)
                    for i in range(1, 4):
                        tile = jnp.where(group == i, left(pieces[i], SUB * (p - i) % 128), tile)
                    at = (4 * m + p) * CH + 16 * h
                    taps[at : at + 16, 128 * half : 128 * half + 128] = tile
    weights = lax.dot_general(
        order, taps[...], (((1,), (1,)), ((), ())), preferred_element_type=F32
    ).astype(BF16)

    spread = lax.broadcasted_iota(jnp.int32, (1, 128), 1)
    norms = jnp.zeros((1, 128), F32)
    for j in range(EVENTS):
        both = [t[j // 2, j % 2].astype(F32) for t in tmpls]
        norm = jnp.sum(sum(b * b for b in both), keepdims=True)
        norms = jnp.where(spread == j, norm, norms)
    rest = jnp.concatenate([norms, jnp.zeros((3, 128), F32)], axis=0)
    for s in range(PLANE):
        side[s, 4:8, :] = rest
    for by in flat:
        to = moved(me, by)
        there = spot(to, ("y", "x"))
        remote(side.at[there], sides.at[here], s_e, r_e, to).start()
    sides[here] = side[here]
    near = steps(("zl", "core"))
    mine = spot(me, ("zl", "core"))

    products = (product0, product1)
    turns = [lax.rem(me["y"] + d, 4) for d in (2, 1, 3, 0)]

    def multiply(i):
        at = pl.multiple_of(turns[i] * CHUNK, CHUNK)
        stack = jnp.concatenate([phases[:, pl.ds(at + 128 * m, CHUNK + 128)] for m in range(4)], axis=0)
        products[i % 2][...] = jnp.dot(weights, stack, preferred_element_type=F32)

    multiply(0)
    for i in range(4):
        if i < 3:
            multiply(i + 1)
        product = products[i % 2]
        total = product[0:8, 0:CHUNK]
        for b in range(1, SUB):
            total = total + left(product[8 * b : 8 * b + 8, :], b)[:, :CHUNK]
        for q in range(4):
            part[turns[i] * 4 + q] = total[:, SPAN * q : SPAN * q + SPAN]
        for dx in (2, 1, 3, 0):
            if i == 3 and dx == 0:
                continue
            to = {"y": turns[i], "x": lax.rem(me["x"] + dx, 4)}
            there = spot(to, ("y", "x"))
            remote(part.at[there], arrived.at[here], s_p, r_p, to).start()
    settle(sides, PLANE - 1, s_e, r_e, beside).wait_recv()
    corner[mine] = jnp.sum(sides[...], axis=0)
    for by in near:
        remote(corner.at[mine], corner.at[mine], s_c, r_c, moved(me, by)).start()
    arrived[here] = part[here]
    settle(arrived, PLANE - 1, s_p, r_p, beside).wait_recv()

    quad[mine] = jnp.sum(arrived[...], axis=0)
    for by in near[::-1]:
        remote(quad.at[mine], quad.at[mine], s_q, r_q, moved(me, by)).start()
    partner = moved(me, near[0])
    settle(corner, 3, s_c, r_c, partner).wait_recv()
    ends = (corner[0] + corner[1]) + (corner[2] + corner[3])
    energy = jnp.concatenate([ends[i : i + 1, :] for i in range(4)], axis=1)
    row = lax.broadcasted_iota(jnp.int32, (EVENTS, 128), 0)
    col = lax.broadcasted_iota(jnp.int32, (EVENTS, 128), 1)
    norm = jnp.sum(jnp.where(row == col, ends[4:5, :], 0.0), axis=1, keepdims=True)
    root = jnp.sqrt(energy * norm + 1e-6)
    settle(sides, PLANE - 1, s_e, r_e, beside).wait_send()
    settle(arrived, PLANE - 1, s_p, r_p, beside).wait_send()
    settle(corner, 3, s_c, r_c, partner).wait_send()
    for h in range(PIECES):
        settle(tmpls[h], 3, s_g.at[h], r_g.at[h], above).wait_send()
        halos[h].wait_send()
    settle(quad, 3, s_q, r_q, partner).wait_recv()
    total = (quad[0] + quad[1]) + (quad[2] + quad[3])
    for i in range(4):
        score_ref[i] = total[2 * i : 2 * i + 2, :]
        root_ref[i] = root[2 * i : 2 * i + 2, :]
    settle(quad, 3, s_q, r_q, partner).wait_send()


def local(record, event_stretch, event_offset):
    dma = pltpu.SemaphoreType.DMA
    blocks = pltpu.VMEM((PLANE, ROWS, SPAN), BF16)
    pairs = pltpu.VMEM((4, 2, ROWS, SPAN), BF16)
    total, root = pl.pallas_call(
        kernel,
        out_shape=(jax.ShapeDtypeStruct((4, 2, SPAN), F32),) * 2,
        in_specs=[pl.BlockSpec(memory_space=pltpu.HBM)] * 3,
        out_specs=(pl.BlockSpec(memory_space=pltpu.VMEM),) * 2,
        scratch_shapes=[blocks] * PIECES
        + [pltpu.VMEM((ROWS, SPAN), BF16)] * PIECES
        + [pairs] * (3 * PIECES)
        + [
            pltpu.VMEM((4 * CH, (PLANE + 1) * SPAN), BF16),
            pltpu.VMEM((SPAN, 256), BF16),
            pltpu.VMEM((256, CHUNK + 128), F32),
            pltpu.VMEM((256, CHUNK + 128), F32),
            pltpu.VMEM((24, SPAN), F32),
            pltpu.VMEM((PLANE, EVENTS, SPAN), F32),
            pltpu.VMEM((PLANE, EVENTS, SPAN), F32),
            pltpu.VMEM((4, EVENTS, SPAN), F32),
            pltpu.VMEM((PLANE, EVENTS, 128), F32),
            pltpu.VMEM((PLANE, EVENTS, 128), F32),
            pltpu.VMEM((4, EVENTS, 128), F32),
        ]
        + [dma((PIECES,))] * 9
        + [dma] * 8
        + [pltpu.SMEM((2, 4), jnp.int32)] * 2
        + [dma((2,))],
        compiler_params=pltpu.CompilerParams(vmem_limit_bytes=56377244, collective_id=0, has_side_effects=True),
        name="matching",
    )(event_stretch.T, event_offset.T, record.reshape(PLANE, CH, SPAN))
    return total / root


def solution(mesh):
    torus = Mesh(mesh.devices.reshape(4, 4, 4, 2, 2), AXES)
    return jax.shard_map(
        local,
        mesh=torus,
        in_specs=(P(("zl", "core"), ("zh", "y", "x")), P(), P()),
        out_specs=P(None, None, ("zh", "y", "x")),
        check_vma=False,
    )
```

```python
import functools
import itertools

import jax
import jax.numpy as jnp
from jax import lax
from jax.experimental import pallas as pl
from jax.experimental.pallas import tpu as pltpu
from jax.sharding import Mesh
from jax.sharding import PartitionSpec as P

TAPS = 500
AXES = ("zh", "y", "x", "zl", "core")
SIZE = {"zh": 4, "y": 4, "x": 4, "zl": 2, "core": 2}
MESH = pl.DeviceIdType.MESH
F32 = jnp.float32
BF16 = jnp.bfloat16
SPAN = 512
PLANE = 16
CH = 32
PIECES = 4
ROWS = CH // PIECES
EVENTS = 8
SUB = 32
CHUNK = 2048


def steps(axes):
    grid = itertools.product(*[range(SIZE[a]) for a in axes])
    return [dict(zip(axes, at)) for at in grid if any(at)]


def moved(me, by, sign=1):
    return {a: lax.rem(me[a] + sign * by[a] + SIZE[a], SIZE[a]) for a in by}


def spot(at, axes):
    index = 0
    for a in axes:
        index = index * SIZE[a] + at[a]
    return index


def remote(src, dst, send, recv, to):
    return pltpu.make_async_remote_copy(
        src_ref=src, dst_ref=dst, send_sem=send, recv_sem=recv, device_id=to, device_id_type=MESH
    )


def greet(me, groups):
    barrier = pltpu.get_barrier_semaphore()
    count = 0
    for axes in groups:
        for by in steps(axes):
            pl.semaphore_signal(barrier, inc=1, device_id=moved(me, by), device_id_type=MESH)
            count += 1
    pl.semaphore_wait(barrier, count)


def left(x, by):
    return pltpu.roll(x, x.shape[1] - by, 1) if by else x


def settle(ref, count, send, recv, to):
    whole = remote(ref.at[pl.ds(0, count)], ref.at[pl.ds(0, count)], send, recv, to)
    return whole


def kernel(
    stretch_hbm,
    offset_hbm,
    x_hbm,
    score_ref,
    root_ref,
    *scratch,
):
    recs, nexts, cands, pickss, tmpls = (scratch[i * PIECES : i * PIECES + PIECES] for i in range(5))
    (
        phases,
        taps,
        product0,
        product1,
        power,
        part,
        arrived,
        quad,
        side,
        sides,
        corner,
        s_xy,
        r_xy,
        s_z,
        r_z,
        s_g,
        r_g,
        s_h,
        r_h,
        own,
        s_p,
        r_p,
        s_q,
        r_q,
        s_e,
        r_e,
        s_c,
        r_c,
        stretch_ref,
        offset_ref,
        r_i,
        x_ref,
        r_x,
    ) = scratch[5 * PIECES :]
    me = {a: lax.axis_index(a) for a in AXES}
    tables = [
        pltpu.make_async_copy(stretch_hbm, stretch_ref, r_i.at[0]),
        pltpu.make_async_copy(offset_hbm, offset_ref, r_i.at[1]),
    ]
    whole = pltpu.make_async_copy(x_hbm, x_ref, r_x)
    whole.start()
    for table in tables:
        table.start()
    greet(me, [("y", "x"), ("zh",), ("zl", "core")])
    whole.wait()
    here = spot(me, ("y", "x"))
    zh = me["zh"]
    flat = steps(("y", "x"))
    beside = moved(me, flat[0])
    above = {"zh": lax.rem(zh + 1, 4)}

    kept = []
    for h in range(PIECES):
        rows = slice(ROWS * h, ROWS * h + ROWS)
        for by in flat:
            to = moved(me, by)
            there = spot(to, ("y", "x"))
            remote(x_ref.at[there, rows], recs[h].at[here], s_xy.at[h], r_xy.at[h], to).start()
        keep = pltpu.make_async_copy(x_ref.at[here, rows], recs[h].at[here], own.at[h])
        keep.start()
        kept.append(keep)

    for table in tables:
        table.wait()

    def pick(h):
        settle(pickss[h], 3, s_z.at[h], r_z.at[h], above).wait_recv()
        for i in range(2):
            wide = pickss[h][lax.div(stretch_ref[i, zh], PLANE), i].astype(F32)
            shift = jnp.full((ROWS, SPAN), offset_ref[i, zh], jnp.int32)
            for bit in (1, 2, 4, 8):
                wide = jnp.where((shift & bit) != 0, left(wide, bit), wide)
            tmpls[h][zh, i] = jnp.where(tap < TAPS, wide, 0.0).astype(BF16)
        for d in (2, 1, 3):
            q = lax.rem(zh + d, 4)
            remote(tmpls[h].at[zh], tmpls[h].at[zh], s_g.at[h], r_g.at[h], {"zh": q}).start()

    back = {"zh": lax.rem(zh + 3, 4)}
    tap = lax.broadcasted_iota(jnp.int32, (ROWS, SPAN), 1)
    halos = []
    for h in range(PIECES):
        rows = slice(ROWS * h, ROWS * h + ROWS)
        kept[h].wait()
        settle(recs[h], PLANE - 1, s_xy.at[h], r_xy.at[h], beside).wait_recv()
        for j in range(EVENTS):
            cands[h][j // 2, j % 2] = recs[h][lax.rem(stretch_ref[j % 2, j // 2], PLANE)]
        for d in (2, 1, 3):
            q = lax.rem(zh + d, 4)
            remote(cands[h].at[q], pickss[h].at[zh], s_z.at[h], r_z.at[h], {"zh": q}).start()
        pickss[h][zh] = cands[h][zh]
    for h in range(PIECES):
        pick(h)
    for h in range(PIECES):
        halo = remote(recs[h].at[0], nexts[h], s_h.at[h], r_h.at[h], back)
        halo.start()
        halos.append(halo)

    def merged(blocks):
        if PIECES == 2:
            return blocks
        return [jnp.concatenate(blocks[i : i + 2], axis=0) for i in (0, 2)]

    def fill(s, here, after):
        total = None
        at = pl.multiple_of(s * SPAN, SPAN)
        here, after = merged(here), merged(after)
        for h in range(2):
            wide = here[h].astype(F32)
            square = jnp.sum(wide * wide, axis=0, keepdims=True)
            total = square if h == 0 else total + square
            joined = jnp.concatenate([here[h], after[h]], axis=1)
            for p in range(4):
                row = p * CH + h * 16
                phases[row : row + 16, pl.ds(at, SPAN)] = left(joined, SUB * p)[:, :SPAN]
        power[pl.ds(s, 1), :] = total

    @pl.loop(0, PLANE - 1)
    def _(s):
        fill(s, [r[s] for r in recs], [r[s + 1, :, 0:128] for r in recs])

    for halo in halos:
        halo.wait_recv()
    inside = (zh < 3).astype(F32)
    follow = [(n[...].astype(F32) * inside).astype(BF16) for n in nexts]
    fill(PLANE - 1, [r[PLANE - 1] for r in recs], [f[:, 0:128] for f in follow])
    fill(PLANE, follow, [jnp.zeros((ROWS, 128), BF16)] * PIECES)
    for h in range(PIECES):
        settle(recs[h], PLANE - 1, s_xy.at[h], r_xy.at[h], beside).wait_send()
        settle(pickss[h], 3, s_z.at[h], r_z.at[h], above).wait_send()

    double = jnp.concatenate([power[0:PLANE, :], power[1 : PLANE + 1, :]], axis=1)
    sums = {1: double}
    for size in (1, 2, 4, 8, 16, 32, 64, 128):
        sums[2 * size] = sums[size] + left(sums[size], size)
    energy = sums[256][:, :SPAN]
    start = 256
    for size in (128, 64, 32, 16, 4):
        energy = energy + left(sums[size], start)[:, :SPAN]
        start += size
    for s in range(PLANE):
        for i in range(4):
            side[s, i : i + 1, :] = energy[s : s + 1, 128 * i : 128 * i + 128]

    row = lax.broadcasted_iota(jnp.int32, (256, 256), 0)
    col = lax.broadcasted_iota(jnp.int32, (256, 256), 1)
    order = (lax.rem(row, 8) * SUB + lax.div(row, 8) == col).astype(F32).astype(BF16)
    group = lax.div(lax.broadcasted_iota(jnp.int32, (16, 128), 1), SUB).astype(F32).astype(BF16)
    for h in range(2):
        for k in range(h * PIECES // 2, (h + 1) * PIECES // 2):
            settle(tmpls[k], 3, s_g.at[k], r_g.at[k], above).wait_recv()
        for half in range(2):
            for m in range(4):
                pieces = [
                    jnp.concatenate(
                        [
                            t[(4 * half + i) // 2, i % 2, :, 128 * m : 128 * m + 128]
                            for t in tmpls[h * PIECES // 2 : (h + 1) * PIECES // 2]
                        ],
                        axis=0,
                    )
                    for i in range(4)
                ]
                for p in range(4):
                    tile = left(pieces[0], SUB * p)
                    for i in range(1, 4):
                        tile = jnp.where(group == i, left(pieces[i], SUB * (p - i) % 128), tile)
                    at = (4 * m + p) * CH + 16 * h
                    taps[at : at + 16, 128 * half : 128 * half + 128] = tile
    weights = lax.dot_general(
        order, taps[...], (((1,), (1,)), ((), ())), preferred_element_type=F32
    ).astype(BF16)

    def tell():
        spread = lax.broadcasted_iota(jnp.int32, (1, 128), 1)
        norms = jnp.zeros((1, 128), F32)
        for j in range(EVENTS):
            both = [t[j // 2, j % 2].astype(F32) for t in tmpls]
            norm = jnp.sum(sum(b * b for b in both), keepdims=True)
            norms = jnp.where(spread == j, norm, norms)
        rest = jnp.concatenate([norms, jnp.zeros((3, 128), F32)], axis=0)
        for s in range(PLANE):
            side[s, 4:8, :] = rest
        for by in flat:
            to = moved(me, by)
            there = spot(to, ("y", "x"))
            remote(side.at[there], sides.at[here], s_e, r_e, to).start()
        sides[here] = side[here]

    near = steps(("zl", "core"))
    mine = spot(me, ("zl", "core"))

    products = (product0, product1)
    turns = [lax.rem(me["y"] + d, 4) for d in (2, 1, 3, 0)]

    def multiply(i):
        at = pl.multiple_of(turns[i] * CHUNK, CHUNK)
        stack = jnp.concatenate([phases[:, pl.ds(at + 128 * m, CHUNK + 128)] for m in range(4)], axis=0)
        products[i % 2][...] = jnp.dot(weights, stack, preferred_element_type=F32)

    multiply(0)
    for i in range(4):
        if i < 3:
            multiply(i + 1)
        product = products[i % 2]
        total = product[0:8, 0:CHUNK]
        for b in range(1, SUB):
            total = total + left(product[8 * b : 8 * b + 8, :], b)[:, :CHUNK]
        for q in range(4):
            part[turns[i] * 4 + q] = total[:, SPAN * q : SPAN * q + SPAN]
        for dx in (2, 1, 3, 0):
            if i == 3 and dx == 0:
                continue
            to = {"y": turns[i], "x": lax.rem(me["x"] + dx, 4)}
            there = spot(to, ("y", "x"))
            remote(part.at[there], arrived.at[here], s_p, r_p, to).start()
        if i == 0:
            tell()
    settle(sides, PLANE - 1, s_e, r_e, beside).wait_recv()
    corner[mine] = jnp.sum(sides[...], axis=0)
    for by in near:
        remote(corner.at[mine], corner.at[mine], s_c, r_c, moved(me, by)).start()
    arrived[here] = part[here]
    settle(arrived, PLANE - 1, s_p, r_p, beside).wait_recv()

    quad[mine] = jnp.sum(arrived[...], axis=0)
    for by in near[::-1]:
        remote(quad.at[mine], quad.at[mine], s_q, r_q, moved(me, by)).start()
    partner = moved(me, near[0])
    settle(corner, 3, s_c, r_c, partner).wait_recv()
    ends = (corner[0] + corner[1]) + (corner[2] + corner[3])
    energy = jnp.concatenate([ends[i : i + 1, :] for i in range(4)], axis=1)
    row = lax.broadcasted_iota(jnp.int32, (EVENTS, 128), 0)
    col = lax.broadcasted_iota(jnp.int32, (EVENTS, 128), 1)
    norm = jnp.sum(jnp.where(row == col, ends[4:5, :], 0.0), axis=1, keepdims=True)
    root = jnp.sqrt(energy * norm + 1e-6)
    settle(sides, PLANE - 1, s_e, r_e, beside).wait_send()
    settle(arrived, PLANE - 1, s_p, r_p, beside).wait_send()
    settle(corner, 3, s_c, r_c, partner).wait_send()
    for h in range(PIECES):
        settle(tmpls[h], 3, s_g.at[h], r_g.at[h], above).wait_send()
        halos[h].wait_send()
    settle(quad, 3, s_q, r_q, partner).wait_recv()
    total = (quad[0] + quad[1]) + (quad[2] + quad[3])
    for i in range(4):
        score_ref[i] = total[2 * i : 2 * i + 2, :]
        root_ref[i] = root[2 * i : 2 * i + 2, :]
    settle(quad, 3, s_q, r_q, partner).wait_send()


def local(record, event_stretch, event_offset):
    dma = pltpu.SemaphoreType.DMA
    blocks = pltpu.VMEM((PLANE, ROWS, SPAN), BF16)
    pairs = pltpu.VMEM((4, 2, ROWS, SPAN), BF16)
    total, root = pl.pallas_call(
        kernel,
        out_shape=(jax.ShapeDtypeStruct((4, 2, SPAN), F32),) * 2,
        in_specs=[pl.BlockSpec(memory_space=pltpu.HBM)] * 3,
        out_specs=(pl.BlockSpec(memory_space=pltpu.VMEM),) * 2,
        scratch_shapes=[blocks] * PIECES
        + [pltpu.VMEM((ROWS, SPAN), BF16)] * PIECES
        + [pairs] * (3 * PIECES)
        + [
            pltpu.VMEM((4 * CH, (PLANE + 1) * SPAN), BF16),
            pltpu.VMEM((SPAN, 256), BF16),
            pltpu.VMEM((256, CHUNK + 128), F32),
            pltpu.VMEM((256, CHUNK + 128), F32),
            pltpu.VMEM((24, SPAN), F32),
            pltpu.VMEM((PLANE, EVENTS, SPAN), F32),
            pltpu.VMEM((PLANE, EVENTS, SPAN), F32),
            pltpu.VMEM((4, EVENTS, SPAN), F32),
            pltpu.VMEM((PLANE, EVENTS, 128), F32),
            pltpu.VMEM((PLANE, EVENTS, 128), F32),
            pltpu.VMEM((4, EVENTS, 128), F32),
        ]
        + [dma((PIECES,))] * 9
        + [dma] * 8
        + [pltpu.SMEM((2, 4), jnp.int32)] * 2
        + [dma((2,)), pltpu.VMEM((PLANE, CH, SPAN), BF16), dma],
        compiler_params=pltpu.CompilerParams(vmem_limit_bytes=56377244, collective_id=0, has_side_effects=True),
        name="matching",
    )(event_stretch.T, event_offset.T, record.reshape(PLANE, CH, SPAN))
    return total / root


def solution(mesh):
    torus = Mesh(mesh.devices.reshape(4, 4, 4, 2, 2), AXES)
    return jax.shard_map(
        local,
        mesh=torus,
        in_specs=(P(("zl", "core"), ("zh", "y", "x")), P(), P()),
        out_specs=P(None, None, ("zh", "y", "x")),
        check_vma=False,
    )
```

```python
import functools
import itertools

import jax
import jax.numpy as jnp
from jax import lax
from jax.experimental import pallas as pl
from jax.experimental.pallas import tpu as pltpu
from jax.sharding import Mesh
from jax.sharding import PartitionSpec as P

TAPS = 500
AXES = ("zh", "y", "x", "zl", "core")
SIZE = {"zh": 4, "y": 4, "x": 4, "zl": 2, "core": 2}
MESH = pl.DeviceIdType.MESH
F32 = jnp.float32
BF16 = jnp.bfloat16
SPAN = 512
PLANE = 16
CH = 32
PIECES = 4
ROWS = CH // PIECES
EVENTS = 8
SUB = 32
CHUNK = 2048


def steps(axes):
    grid = itertools.product(*[range(SIZE[a]) for a in axes])
    return [dict(zip(axes, at)) for at in grid if any(at)]


def moved(me, by, sign=1):
    return {a: lax.rem(me[a] + sign * by[a] + SIZE[a], SIZE[a]) for a in by}


def spot(at, axes):
    index = 0
    for a in axes:
        index = index * SIZE[a] + at[a]
    return index


def remote(src, dst, send, recv, to):
    return pltpu.make_async_remote_copy(
        src_ref=src, dst_ref=dst, send_sem=send, recv_sem=recv, device_id=to, device_id_type=MESH
    )


def greet(me, groups):
    barrier = pltpu.get_barrier_semaphore()
    count = 0
    for axes in groups:
        for by in steps(axes):
            pl.semaphore_signal(barrier, inc=1, device_id=moved(me, by), device_id_type=MESH)
            count += 1
    pl.semaphore_wait(barrier, count)


def left(x, by):
    return pltpu.roll(x, x.shape[1] - by, 1) if by else x


def settle(ref, count, send, recv, to):
    whole = remote(ref.at[pl.ds(0, count)], ref.at[pl.ds(0, count)], send, recv, to)
    return whole


def kernel(
    stretch_hbm,
    offset_hbm,
    x_hbm,
    score_ref,
    root_ref,
    *scratch,
):
    recs, nexts, cands, pickss, tmpls = (scratch[i * PIECES : i * PIECES + PIECES] for i in range(5))
    (
        phases,
        taps,
        product0,
        product1,
        power,
        part,
        arrived,
        quad,
        side,
        sides,
        corner,
        s_xy,
        r_xy,
        s_z,
        r_z,
        s_g,
        r_g,
        s_h,
        r_h,
        own,
        s_p,
        r_p,
        s_q,
        r_q,
        s_e,
        r_e,
        s_c,
        r_c,
        stretch_ref,
        offset_ref,
        r_i,
        x_ref,
        r_x,
    ) = scratch[5 * PIECES :]
    me = {a: lax.axis_index(a) for a in AXES}
    tables = [
        pltpu.make_async_copy(stretch_hbm, stretch_ref, r_i.at[0]),
        pltpu.make_async_copy(offset_hbm, offset_ref, r_i.at[1]),
    ]
    whole = pltpu.make_async_copy(x_hbm, x_ref, r_x)
    whole.start()
    for table in tables:
        table.start()
    greet(me, [("zh",), ("y", "x"), ("zl", "core")])
    whole.wait()
    here = spot(me, ("y", "x"))
    zh = me["zh"]
    flat = steps(("y", "x"))
    beside = moved(me, flat[0])
    above = {"zh": lax.rem(zh + 1, 4)}

    kept = []
    for h in range(PIECES):
        rows = slice(ROWS * h, ROWS * h + ROWS)
        for by in flat:
            to = moved(me, by)
            there = spot(to, ("y", "x"))
            remote(x_ref.at[there, rows], recs[h].at[here], s_xy.at[h], r_xy.at[h], to).start()
        keep = pltpu.make_async_copy(x_ref.at[here, rows], recs[h].at[here], own.at[h])
        keep.start()
        kept.append(keep)

    for table in tables:
        table.wait()

    def pick(h):
        settle(pickss[h], 3, s_z.at[h], r_z.at[h], above).wait_recv()
        for i in range(2):
            wide = pickss[h][lax.div(stretch_ref[i, zh], PLANE), i].astype(F32)
            shift = jnp.full((ROWS, SPAN), offset_ref[i, zh], jnp.int32)
            for bit in (1, 2, 4, 8):
                wide = jnp.where((shift & bit) != 0, left(wide, bit), wide)
            tmpls[h][zh, i] = jnp.where(tap < TAPS, wide, 0.0).astype(BF16)
        for d in (2, 1, 3):
            q = lax.rem(zh + d, 4)
            remote(tmpls[h].at[zh], tmpls[h].at[zh], s_g.at[h], r_g.at[h], {"zh": q}).start()

    back = {"zh": lax.rem(zh + 3, 4)}
    tap = lax.broadcasted_iota(jnp.int32, (ROWS, SPAN), 1)
    halos = []
    for h in range(PIECES):
        rows = slice(ROWS * h, ROWS * h + ROWS)
        kept[h].wait()
        settle(recs[h], PLANE - 1, s_xy.at[h], r_xy.at[h], beside).wait_recv()
        for j in range(EVENTS):
            cands[h][j // 2, j % 2] = recs[h][lax.rem(stretch_ref[j % 2, j // 2], PLANE)]
        for d in (2, 1, 3):
            q = lax.rem(zh + d, 4)
            remote(cands[h].at[q], pickss[h].at[zh], s_z.at[h], r_z.at[h], {"zh": q}).start()
        pickss[h][zh] = cands[h][zh]
    for h in range(PIECES):
        pick(h)
    for h in range(PIECES):
        halo = remote(recs[h].at[0], nexts[h], s_h.at[h], r_h.at[h], back)
        halo.start()
        halos.append(halo)

    def merged(blocks):
        if PIECES == 2:
            return blocks
        return [jnp.concatenate(blocks[i : i + 2], axis=0) for i in (0, 2)]

    def fill(s, here, after):
        total = None
        at = pl.multiple_of(s * SPAN, SPAN)
        here, after = merged(here), merged(after)
        for h in range(2):
            wide = here[h].astype(F32)
            square = jnp.sum(wide * wide, axis=0, keepdims=True)
            total = square if h == 0 else total + square
            joined = jnp.concatenate([here[h], after[h]], axis=1)
            for p in range(4):
                row = p * CH + h * 16
                phases[row : row + 16, pl.ds(at, SPAN)] = left(joined, SUB * p)[:, :SPAN]
        power[pl.ds(s, 1), :] = total

    @pl.loop(0, PLANE - 1)
    def _(s):
        fill(s, [r[s] for r in recs], [r[s + 1, :, 0:128] for r in recs])

    for halo in halos:
        halo.wait_recv()
    inside = (zh < 3).astype(F32)
    follow = [(n[...].astype(F32) * inside).astype(BF16) for n in nexts]
    fill(PLANE - 1, [r[PLANE - 1] for r in recs], [f[:, 0:128] for f in follow])
    fill(PLANE, follow, [jnp.zeros((ROWS, 128), BF16)] * PIECES)
    for h in range(PIECES):
        settle(recs[h], PLANE - 1, s_xy.at[h], r_xy.at[h], beside).wait_send()
        settle(pickss[h], 3, s_z.at[h], r_z.at[h], above).wait_send()

    double = jnp.concatenate([power[0:PLANE, :], power[1 : PLANE + 1, :]], axis=1)
    sums = {1: double}
    for size in (1, 2, 4, 8, 16, 32, 64, 128):
        sums[2 * size] = sums[size] + left(sums[size], size)
    energy = sums[256][:, :SPAN]
    start = 256
    for size in (128, 64, 32, 16, 4):
        energy = energy + left(sums[size], start)[:, :SPAN]
        start += size
    for s in range(PLANE):
        for i in range(4):
            side[s, i : i + 1, :] = energy[s : s + 1, 128 * i : 128 * i + 128]

    row = lax.broadcasted_iota(jnp.int32, (256, 256), 0)
    col = lax.broadcasted_iota(jnp.int32, (256, 256), 1)
    order = (lax.rem(row, 8) * SUB + lax.div(row, 8) == col).astype(F32).astype(BF16)
    group = lax.div(lax.broadcasted_iota(jnp.int32, (16, 128), 1), SUB).astype(F32).astype(BF16)
    for h in range(2):
        for k in range(h * PIECES // 2, (h + 1) * PIECES // 2):
            settle(tmpls[k], 3, s_g.at[k], r_g.at[k], above).wait_recv()
        for half in range(2):
            for m in range(4):
                pieces = [
                    jnp.concatenate(
                        [
                            t[(4 * half + i) // 2, i % 2, :, 128 * m : 128 * m + 128]
                            for t in tmpls[h * PIECES // 2 : (h + 1) * PIECES // 2]
                        ],
                        axis=0,
                    )
                    for i in range(4)
                ]
                for p in range(4):
                    tile = left(pieces[0], SUB * p)
                    for i in range(1, 4):
                        tile = jnp.where(group == i, left(pieces[i], SUB * (p - i) % 128), tile)
                    at = (4 * m + p) * CH + 16 * h
                    taps[at : at + 16, 128 * half : 128 * half + 128] = tile
    weights = lax.dot_general(
        order, taps[...], (((1,), (1,)), ((), ())), preferred_element_type=F32
    ).astype(BF16)

    def tell():
        spread = lax.broadcasted_iota(jnp.int32, (1, 128), 1)
        norms = jnp.zeros((1, 128), F32)
        for j in range(EVENTS):
            both = [t[j // 2, j % 2].astype(F32) for t in tmpls]
            norm = jnp.sum(sum(b * b for b in both), keepdims=True)
            norms = jnp.where(spread == j, norm, norms)
        rest = jnp.concatenate([norms, jnp.zeros((3, 128), F32)], axis=0)
        for s in range(PLANE):
            side[s, 4:8, :] = rest
        for by in flat:
            to = moved(me, by)
            there = spot(to, ("y", "x"))
            remote(side.at[there], sides.at[here], s_e, r_e, to).start()
        sides[here] = side[here]

    near = steps(("zl", "core"))
    mine = spot(me, ("zl", "core"))

    products = (product0, product1)
    turns = [lax.rem(me["y"] + d, 4) for d in (2, 1, 3, 0)]

    def multiply(i):
        at = pl.multiple_of(turns[i] * CHUNK, CHUNK)
        stack = jnp.concatenate([phases[:, pl.ds(at + 128 * m, CHUNK + 128)] for m in range(4)], axis=0)
        products[i % 2][...] = jnp.dot(weights, stack, preferred_element_type=F32)

    multiply(0)
    for i in range(4):
        if i < 3:
            multiply(i + 1)
        product = products[i % 2]
        total = product[0:8, 0:CHUNK]
        for b in range(1, SUB):
            total = total + left(product[8 * b : 8 * b + 8, :], b)[:, :CHUNK]
        for q in range(4):
            part[turns[i] * 4 + q] = total[:, SPAN * q : SPAN * q + SPAN]
        for dx in (2, 1, 3, 0):
            if i == 3 and dx == 0:
                continue
            to = {"y": turns[i], "x": lax.rem(me["x"] + dx, 4)}
            there = spot(to, ("y", "x"))
            remote(part.at[there], arrived.at[here], s_p, r_p, to).start()
        if i == 0:
            tell()
    settle(sides, PLANE - 1, s_e, r_e, beside).wait_recv()
    corner[mine] = jnp.sum(sides[...], axis=0)
    for by in near:
        remote(corner.at[mine], corner.at[mine], s_c, r_c, moved(me, by)).start()
    arrived[here] = part[here]
    settle(arrived, PLANE - 1, s_p, r_p, beside).wait_recv()

    quad[mine] = jnp.sum(arrived[...], axis=0)
    for by in near[::-1]:
        remote(quad.at[mine], quad.at[mine], s_q, r_q, moved(me, by)).start()
    partner = moved(me, near[0])
    settle(corner, 3, s_c, r_c, partner).wait_recv()
    ends = (corner[0] + corner[1]) + (corner[2] + corner[3])
    energy = jnp.concatenate([ends[i : i + 1, :] for i in range(4)], axis=1)
    row = lax.broadcasted_iota(jnp.int32, (EVENTS, 128), 0)
    col = lax.broadcasted_iota(jnp.int32, (EVENTS, 128), 1)
    norm = jnp.sum(jnp.where(row == col, ends[4:5, :], 0.0), axis=1, keepdims=True)
    root = jnp.sqrt(energy * norm + 1e-6)
    settle(sides, PLANE - 1, s_e, r_e, beside).wait_send()
    settle(arrived, PLANE - 1, s_p, r_p, beside).wait_send()
    settle(corner, 3, s_c, r_c, partner).wait_send()
    for h in range(PIECES):
        settle(tmpls[h], 3, s_g.at[h], r_g.at[h], above).wait_send()
        halos[h].wait_send()
    settle(quad, 3, s_q, r_q, partner).wait_recv()
    total = (quad[0] + quad[1]) + (quad[2] + quad[3])
    for i in range(4):
        score_ref[i] = total[2 * i : 2 * i + 2, :]
        root_ref[i] = root[2 * i : 2 * i + 2, :]
    settle(quad, 3, s_q, r_q, partner).wait_send()


def pinned(x):
    return pltpu.with_memory_space_constraint(x, pltpu.HBM)


def local(record, event_stretch, event_offset):
    dma = pltpu.SemaphoreType.DMA
    blocks = pltpu.VMEM((PLANE, ROWS, SPAN), BF16)
    pairs = pltpu.VMEM((4, 2, ROWS, SPAN), BF16)
    total, root = pl.pallas_call(
        kernel,
        out_shape=(jax.ShapeDtypeStruct((4, 2, SPAN), F32),) * 2,
        in_specs=[pl.BlockSpec(memory_space=pltpu.HBM)] * 3,
        out_specs=(pl.BlockSpec(memory_space=pltpu.VMEM),) * 2,
        scratch_shapes=[blocks] * PIECES
        + [pltpu.VMEM((ROWS, SPAN), BF16)] * PIECES
        + [pairs] * (3 * PIECES)
        + [
            pltpu.VMEM((4 * CH, (PLANE + 1) * SPAN), BF16),
            pltpu.VMEM((SPAN, 256), BF16),
            pltpu.VMEM((256, CHUNK + 128), F32),
            pltpu.VMEM((256, CHUNK + 128), F32),
            pltpu.VMEM((24, SPAN), F32),
            pltpu.VMEM((PLANE, EVENTS, SPAN), F32),
            pltpu.VMEM((PLANE, EVENTS, SPAN), F32),
            pltpu.VMEM((4, EVENTS, SPAN), F32),
            pltpu.VMEM((PLANE, EVENTS, 128), F32),
            pltpu.VMEM((PLANE, EVENTS, 128), F32),
            pltpu.VMEM((4, EVENTS, 128), F32),
        ]
        + [dma((PIECES,))] * 9
        + [dma] * 8
        + [pltpu.SMEM((2, 4), jnp.int32)] * 2
        + [dma((2,)), pltpu.VMEM((PLANE, CH, SPAN), BF16), dma],
        compiler_params=pltpu.CompilerParams(vmem_limit_bytes=56377244, collective_id=0, has_side_effects=True),
        name="matching",
    )(pinned(event_stretch.T), pinned(event_offset.T), record.reshape(PLANE, CH, SPAN))
    return total / root


def solution(mesh):
    torus = Mesh(mesh.devices.reshape(4, 4, 4, 2, 2), AXES)
    return jax.shard_map(
        local,
        mesh=torus,
        in_specs=(P(("zl", "core"), ("zh", "y", "x")), P(), P()),
        out_specs=P(None, None, ("zh", "y", "x")),
        check_vma=False,
    )
```

```python
import functools
import itertools

import jax
import jax.numpy as jnp
from jax import lax
from jax.experimental import pallas as pl
from jax.experimental.pallas import tpu as pltpu
from jax.sharding import Mesh
from jax.sharding import PartitionSpec as P

TAPS = 500
AXES = ("zh", "y", "x", "zl", "core")
SIZE = {"zh": 4, "y": 4, "x": 4, "zl": 2, "core": 2}
MESH = pl.DeviceIdType.MESH
F32 = jnp.float32
BF16 = jnp.bfloat16
SPAN = 512
PLANE = 16
CH = 32
PIECES = 4
ROWS = CH // PIECES
EVENTS = 8
SUB = 32
CHUNK = 2048


def steps(axes):
    grid = itertools.product(*[range(SIZE[a]) for a in axes])
    return [dict(zip(axes, at)) for at in grid if any(at)]


def moved(me, by, sign=1):
    return {a: lax.rem(me[a] + sign * by[a] + SIZE[a], SIZE[a]) for a in by}


def spot(at, axes):
    index = 0
    for a in axes:
        index = index * SIZE[a] + at[a]
    return index


def remote(src, dst, send, recv, to):
    return pltpu.make_async_remote_copy(
        src_ref=src, dst_ref=dst, send_sem=send, recv_sem=recv, device_id=to, device_id_type=MESH
    )


def greet(me, groups):
    barrier = pltpu.get_barrier_semaphore()
    count = 0
    for axes in groups:
        for by in steps(axes):
            pl.semaphore_signal(barrier, inc=1, device_id=moved(me, by), device_id_type=MESH)
            count += 1
    pl.semaphore_wait(barrier, count)


def left(x, by):
    return pltpu.roll(x, x.shape[1] - by, 1) if by else x


def settle(ref, count, send, recv, to):
    whole = remote(ref.at[pl.ds(0, count)], ref.at[pl.ds(0, count)], send, recv, to)
    return whole


def kernel(
    stretch_hbm,
    offset_hbm,
    x_hbm,
    score_ref,
    root_ref,
    *scratch,
):
    recs, nexts, cands, pickss, tmpls = (scratch[i * PIECES : i * PIECES + PIECES] for i in range(5))
    (
        phases,
        taps,
        product0,
        product1,
        power,
        part,
        arrived,
        quad,
        side,
        sides,
        corner,
        s_xy,
        r_xy,
        s_z,
        r_z,
        s_g,
        r_g,
        s_h,
        r_h,
        own,
        s_p,
        r_p,
        s_q,
        r_q,
        s_e,
        r_e,
        s_c,
        r_c,
        stretch_ref,
        offset_ref,
        r_i,
        x_ref,
        r_x,
    ) = scratch[5 * PIECES :]
    me = {a: lax.axis_index(a) for a in AXES}
    tables = [
        pltpu.make_async_copy(stretch_hbm, stretch_ref, r_i.at[0]),
        pltpu.make_async_copy(offset_hbm, offset_ref, r_i.at[1]),
    ]
    whole = pltpu.make_async_copy(x_hbm, x_ref, r_x)
    whole.start()
    for table in tables:
        table.start()
    greet(me, [("zh",), ("y", "x"), ("zl", "core")])
    whole.wait()
    here = spot(me, ("y", "x"))
    zh = me["zh"]
    flat = steps(("y", "x"))
    beside = moved(me, flat[0])
    above = {"zh": lax.rem(zh + 1, 4)}

    kept = []
    for h in range(PIECES):
        rows = slice(ROWS * h, ROWS * h + ROWS)
        for by in flat:
            to = moved(me, by)
            there = spot(to, ("y", "x"))
            remote(x_ref.at[there, rows], recs[h].at[here], s_xy.at[h], r_xy.at[h], to).start()
        keep = pltpu.make_async_copy(x_ref.at[here, rows], recs[h].at[here], own.at[h])
        keep.start()
        kept.append(keep)

    for table in tables:
        table.wait()

    def pick(h):
        settle(pickss[h], 3, s_z.at[h], r_z.at[h], above).wait_recv()
        for i in range(2):
            wide = pickss[h][lax.div(stretch_ref[i, zh], PLANE), i].astype(F32)
            shift = jnp.full((ROWS, SPAN), offset_ref[i, zh], jnp.int32)
            for bit in (1, 2, 4, 8):
                wide = jnp.where((shift & bit) != 0, left(wide, bit), wide)
            tmpls[h][zh, i] = jnp.where(tap < TAPS, wide, 0.0).astype(BF16)
        for d in (1, 3, 2):
            q = lax.rem(zh + d, 4)
            remote(tmpls[h].at[zh], tmpls[h].at[zh], s_g.at[h], r_g.at[h], {"zh": q}).start()

    back = {"zh": lax.rem(zh + 3, 4)}
    tap = lax.broadcasted_iota(jnp.int32, (ROWS, SPAN), 1)
    halos = []
    for h in range(PIECES):
        rows = slice(ROWS * h, ROWS * h + ROWS)
        kept[h].wait()
        settle(recs[h], PLANE - 1, s_xy.at[h], r_xy.at[h], beside).wait_recv()
        for j in range(EVENTS):
            cands[h][j // 2, j % 2] = recs[h][lax.rem(stretch_ref[j % 2, j // 2], PLANE)]
        for d in (2, 1, 3):
            q = lax.rem(zh + d, 4)
            remote(cands[h].at[q], pickss[h].at[zh], s_z.at[h], r_z.at[h], {"zh": q}).start()
        pickss[h][zh] = cands[h][zh]
    for h in range(PIECES):
        pick(h)
    for h in range(PIECES):
        halo = remote(recs[h].at[0], nexts[h], s_h.at[h], r_h.at[h], back)
        halo.start()
        halos.append(halo)

    def merged(blocks):
        if PIECES == 2:
            return blocks
        return [jnp.concatenate(blocks[i : i + 2], axis=0) for i in (0, 2)]

    def fill(s, here, after):
        total = None
        at = pl.multiple_of(s * SPAN, SPAN)
        here, after = merged(here), merged(after)
        for h in range(2):
            wide = here[h].astype(F32)
            square = jnp.sum(wide * wide, axis=0, keepdims=True)
            total = square if h == 0 else total + square
            joined = jnp.concatenate([here[h], after[h]], axis=1)
            for p in range(4):
                row = p * CH + h * 16
                phases[row : row + 16, pl.ds(at, SPAN)] = left(joined, SUB * p)[:, :SPAN]
        power[pl.ds(s, 1), :] = total

    @pl.loop(0, PLANE - 1)
    def _(s):
        fill(s, [r[s] for r in recs], [r[s + 1, :, 0:128] for r in recs])

    for halo in halos:
        halo.wait_recv()
    inside = (zh < 3).astype(F32)
    follow = [(n[...].astype(F32) * inside).astype(BF16) for n in nexts]
    fill(PLANE - 1, [r[PLANE - 1] for r in recs], [f[:, 0:128] for f in follow])
    fill(PLANE, follow, [jnp.zeros((ROWS, 128), BF16)] * PIECES)
    for h in range(PIECES):
        settle(recs[h], PLANE - 1, s_xy.at[h], r_xy.at[h], beside).wait_send()
        settle(pickss[h], 3, s_z.at[h], r_z.at[h], above).wait_send()

    double = jnp.concatenate([power[0:PLANE, :], power[1 : PLANE + 1, :]], axis=1)
    sums = {1: double}
    for size in (1, 2, 4, 8, 16, 32, 64, 128):
        sums[2 * size] = sums[size] + left(sums[size], size)
    energy = sums[256][:, :SPAN]
    start = 256
    for size in (128, 64, 32, 16, 4):
        energy = energy + left(sums[size], start)[:, :SPAN]
        start += size
    for s in range(PLANE):
        for i in range(4):
            side[s, i : i + 1, :] = energy[s : s + 1, 128 * i : 128 * i + 128]

    row = lax.broadcasted_iota(jnp.int32, (256, 256), 0)
    col = lax.broadcasted_iota(jnp.int32, (256, 256), 1)
    order = (lax.rem(row, 8) * SUB + lax.div(row, 8) == col).astype(F32).astype(BF16)
    group = lax.div(lax.broadcasted_iota(jnp.int32, (16, 128), 1), SUB).astype(F32).astype(BF16)
    for h in range(2):
        for k in range(h * PIECES // 2, (h + 1) * PIECES // 2):
            settle(tmpls[k], 3, s_g.at[k], r_g.at[k], above).wait_recv()
        for half in range(2):
            for m in range(4):
                pieces = [
                    jnp.concatenate(
                        [
                            t[(4 * half + i) // 2, i % 2, :, 128 * m : 128 * m + 128]
                            for t in tmpls[h * PIECES // 2 : (h + 1) * PIECES // 2]
                        ],
                        axis=0,
                    )
                    for i in range(4)
                ]
                for p in range(4):
                    tile = left(pieces[0], SUB * p)
                    for i in range(1, 4):
                        tile = jnp.where(group == i, left(pieces[i], SUB * (p - i) % 128), tile)
                    at = (4 * m + p) * CH + 16 * h
                    taps[at : at + 16, 128 * half : 128 * half + 128] = tile
    weights = lax.dot_general(
        order, taps[...], (((1,), (1,)), ((), ())), preferred_element_type=F32
    ).astype(BF16)

    def tell():
        spread = lax.broadcasted_iota(jnp.int32, (1, 128), 1)
        norms = jnp.zeros((1, 128), F32)
        for j in range(EVENTS):
            both = [t[j // 2, j % 2].astype(F32) for t in tmpls]
            norm = jnp.sum(sum(b * b for b in both), keepdims=True)
            norms = jnp.where(spread == j, norm, norms)
        rest = jnp.concatenate([norms, jnp.zeros((3, 128), F32)], axis=0)
        for s in range(PLANE):
            side[s, 4:8, :] = rest
        for by in flat:
            to = moved(me, by)
            there = spot(to, ("y", "x"))
            remote(side.at[there], sides.at[here], s_e, r_e, to).start()
        sides[here] = side[here]

    near = steps(("zl", "core"))
    mine = spot(me, ("zl", "core"))

    products = (product0, product1)
    turns = [lax.rem(me["y"] + d, 4) for d in (2, 1, 3, 0)]

    def multiply(i):
        at = pl.multiple_of(turns[i] * CHUNK, CHUNK)
        stack = jnp.concatenate([phases[:, pl.ds(at + 128 * m, CHUNK + 128)] for m in range(4)], axis=0)
        products[i % 2][...] = jnp.dot(weights, stack, preferred_element_type=F32)

    multiply(0)
    for i in range(4):
        if i < 3:
            multiply(i + 1)
        product = products[i % 2]
        total = product[0:8, 0:CHUNK]
        for b in range(1, SUB):
            total = total + left(product[8 * b : 8 * b + 8, :], b)[:, :CHUNK]
        for q in range(4):
            part[turns[i] * 4 + q] = total[:, SPAN * q : SPAN * q + SPAN]
        for dx in (2, 1, 3, 0):
            if i == 3 and dx == 0:
                continue
            to = {"y": turns[i], "x": lax.rem(me["x"] + dx, 4)}
            there = spot(to, ("y", "x"))
            remote(part.at[there], arrived.at[here], s_p, r_p, to).start()
        if i == 0:
            tell()
    settle(sides, PLANE - 1, s_e, r_e, beside).wait_recv()
    corner[mine] = jnp.sum(sides[...], axis=0)
    for by in near:
        remote(corner.at[mine], corner.at[mine], s_c, r_c, moved(me, by)).start()
    arrived[here] = part[here]
    settle(arrived, PLANE - 1, s_p, r_p, beside).wait_recv()

    quad[mine] = jnp.sum(arrived[...], axis=0)
    for by in near[::-1]:
        remote(quad.at[mine], quad.at[mine], s_q, r_q, moved(me, by)).start()
    partner = moved(me, near[0])
    settle(corner, 3, s_c, r_c, partner).wait_recv()
    ends = (corner[0] + corner[1]) + (corner[2] + corner[3])
    energy = jnp.concatenate([ends[i : i + 1, :] for i in range(4)], axis=1)
    row = lax.broadcasted_iota(jnp.int32, (EVENTS, 128), 0)
    col = lax.broadcasted_iota(jnp.int32, (EVENTS, 128), 1)
    norm = jnp.sum(jnp.where(row == col, ends[4:5, :], 0.0), axis=1, keepdims=True)
    root = jnp.sqrt(energy * norm + 1e-6)
    settle(sides, PLANE - 1, s_e, r_e, beside).wait_send()
    settle(arrived, PLANE - 1, s_p, r_p, beside).wait_send()
    settle(corner, 3, s_c, r_c, partner).wait_send()
    for h in range(PIECES):
        settle(tmpls[h], 3, s_g.at[h], r_g.at[h], above).wait_send()
        halos[h].wait_send()
    settle(quad, 3, s_q, r_q, partner).wait_recv()
    total = (quad[0] + quad[1]) + (quad[2] + quad[3])
    for i in range(4):
        score_ref[i] = total[2 * i : 2 * i + 2, :]
        root_ref[i] = root[2 * i : 2 * i + 2, :]
    settle(quad, 3, s_q, r_q, partner).wait_send()


def pinned(x):
    return pltpu.with_memory_space_constraint(x, pltpu.HBM)


def local(record, event_stretch, event_offset):
    dma = pltpu.SemaphoreType.DMA
    blocks = pltpu.VMEM((PLANE, ROWS, SPAN), BF16)
    pairs = pltpu.VMEM((4, 2, ROWS, SPAN), BF16)
    total, root = pl.pallas_call(
        kernel,
        out_shape=(jax.ShapeDtypeStruct((4, 2, SPAN), F32),) * 2,
        in_specs=[pl.BlockSpec(memory_space=pltpu.HBM)] * 3,
        out_specs=(pl.BlockSpec(memory_space=pltpu.VMEM),) * 2,
        scratch_shapes=[blocks] * PIECES
        + [pltpu.VMEM((ROWS, SPAN), BF16)] * PIECES
        + [pairs] * (3 * PIECES)
        + [
            pltpu.VMEM((4 * CH, (PLANE + 1) * SPAN), BF16),
            pltpu.VMEM((SPAN, 256), BF16),
            pltpu.VMEM((256, CHUNK + 128), F32),
            pltpu.VMEM((256, CHUNK + 128), F32),
            pltpu.VMEM((24, SPAN), F32),
            pltpu.VMEM((PLANE, EVENTS, SPAN), F32),
            pltpu.VMEM((PLANE, EVENTS, SPAN), F32),
            pltpu.VMEM((4, EVENTS, SPAN), F32),
            pltpu.VMEM((PLANE, EVENTS, 128), F32),
            pltpu.VMEM((PLANE, EVENTS, 128), F32),
            pltpu.VMEM((4, EVENTS, 128), F32),
        ]
        + [dma((PIECES,))] * 9
        + [dma] * 8
        + [pltpu.SMEM((2, 4), jnp.int32)] * 2
        + [dma((2,)), pltpu.VMEM((PLANE, CH, SPAN), BF16), dma],
        compiler_params=pltpu.CompilerParams(vmem_limit_bytes=56377244, collective_id=0, has_side_effects=True),
        name="matching",
    )(pinned(event_stretch.T), pinned(event_offset.T), record.reshape(PLANE, CH, SPAN))
    return total / root


def solution(mesh):
    torus = Mesh(mesh.devices.reshape(4, 4, 4, 2, 2), AXES)
    return jax.shard_map(
        local,
        mesh=torus,
        in_specs=(P(("zl", "core"), ("zh", "y", "x")), P(), P()),
        out_specs=P(None, None, ("zh", "y", "x")),
        check_vma=False,
    )
```

```python
import functools
import itertools

import jax
import jax.numpy as jnp
from jax import lax
from jax.experimental import pallas as pl
from jax.experimental.pallas import tpu as pltpu
from jax.sharding import Mesh
from jax.sharding import PartitionSpec as P

TAPS = 500
AXES = ("zh", "y", "x", "zl", "core")
SIZE = {"zh": 4, "y": 4, "x": 4, "zl": 2, "core": 2}
MESH = pl.DeviceIdType.MESH
F32 = jnp.float32
BF16 = jnp.bfloat16
SPAN = 512
PLANE = 16
CH = 32
PIECES = 4
ROWS = CH // PIECES
EVENTS = 8
SUB = 32
CHUNK = 2048


def steps(axes):
    grid = itertools.product(*[range(SIZE[a]) for a in axes])
    return [dict(zip(axes, at)) for at in grid if any(at)]


def moved(me, by, sign=1):
    return {a: lax.rem(me[a] + sign * by[a] + SIZE[a], SIZE[a]) for a in by}


def spot(at, axes):
    index = 0
    for a in axes:
        index = index * SIZE[a] + at[a]
    return index


def remote(src, dst, send, recv, to):
    return pltpu.make_async_remote_copy(
        src_ref=src, dst_ref=dst, send_sem=send, recv_sem=recv, device_id=to, device_id_type=MESH
    )


def greet(me, groups):
    barrier = pltpu.get_barrier_semaphore()
    count = 0
    for axes in groups:
        for by in sorted(steps(axes), key=lambda by: by.get("zh") != 2):
            pl.semaphore_signal(barrier, inc=1, device_id=moved(me, by), device_id_type=MESH)
            count += 1
    pl.semaphore_wait(barrier, count)


def left(x, by):
    return pltpu.roll(x, x.shape[1] - by, 1) if by else x


def settle(ref, count, send, recv, to):
    whole = remote(ref.at[pl.ds(0, count)], ref.at[pl.ds(0, count)], send, recv, to)
    return whole


def kernel(
    stretch_hbm,
    offset_hbm,
    x_hbm,
    score_ref,
    root_ref,
    *scratch,
):
    recs, nexts, cands, pickss, tmpls = (scratch[i * PIECES : i * PIECES + PIECES] for i in range(5))
    (
        phases,
        taps,
        product0,
        product1,
        power,
        part,
        arrived,
        quad,
        side,
        sides,
        corner,
        s_xy,
        r_xy,
        s_z,
        r_z,
        s_g,
        r_g,
        s_h,
        r_h,
        own,
        s_p,
        r_p,
        s_q,
        r_q,
        s_e,
        r_e,
        s_c,
        r_c,
        stretch_ref,
        offset_ref,
        r_i,
        x_ref,
        r_x,
    ) = scratch[5 * PIECES :]
    me = {a: lax.axis_index(a) for a in AXES}
    tables = [
        pltpu.make_async_copy(stretch_hbm, stretch_ref, r_i.at[0]),
        pltpu.make_async_copy(offset_hbm, offset_ref, r_i.at[1]),
    ]
    whole = pltpu.make_async_copy(x_hbm, x_ref, r_x)
    whole.start()
    for table in tables:
        table.start()
    greet(me, [("zh",), ("y", "x"), ("zl", "core")])
    whole.wait()
    here = spot(me, ("y", "x"))
    zh = me["zh"]
    flat = steps(("y", "x"))
    beside = moved(me, flat[0])
    above = {"zh": lax.rem(zh + 1, 4)}

    kept = []
    for h in range(PIECES):
        rows = slice(ROWS * h, ROWS * h + ROWS)
        for by in flat:
            to = moved(me, by)
            there = spot(to, ("y", "x"))
            remote(x_ref.at[there, rows], recs[h].at[here], s_xy.at[h], r_xy.at[h], to).start()
        keep = pltpu.make_async_copy(x_ref.at[here, rows], recs[h].at[here], own.at[h])
        keep.start()
        kept.append(keep)

    for table in tables:
        table.wait()

    def pick(h):
        settle(pickss[h], 3, s_z.at[h], r_z.at[h], above).wait_recv()
        for i in range(2):
            wide = pickss[h][lax.div(stretch_ref[i, zh], PLANE), i].astype(F32)
            shift = jnp.full((ROWS, SPAN), offset_ref[i, zh], jnp.int32)
            for bit in (1, 2, 4, 8):
                wide = jnp.where((shift & bit) != 0, left(wide, bit), wide)
            tmpls[h][zh, i] = jnp.where(tap < TAPS, wide, 0.0).astype(BF16)
        for d in (1, 3, 2):
            q = lax.rem(zh + d, 4)
            remote(tmpls[h].at[zh], tmpls[h].at[zh], s_g.at[h], r_g.at[h], {"zh": q}).start()

    back = {"zh": lax.rem(zh + 3, 4)}
    tap = lax.broadcasted_iota(jnp.int32, (ROWS, SPAN), 1)
    halos = []
    for h in range(PIECES):
        rows = slice(ROWS * h, ROWS * h + ROWS)
        kept[h].wait()
        settle(recs[h], PLANE - 1, s_xy.at[h], r_xy.at[h], beside).wait_recv()
        for j in range(EVENTS):
            cands[h][j // 2, j % 2] = recs[h][lax.rem(stretch_ref[j % 2, j // 2], PLANE)]
        for d in (2, 1, 3):
            q = lax.rem(zh + d, 4)
            remote(cands[h].at[q], pickss[h].at[zh], s_z.at[h], r_z.at[h], {"zh": q}).start()
        pickss[h][zh] = cands[h][zh]
    for h in range(PIECES):
        pick(h)
    for h in range(PIECES):
        halo = remote(recs[h].at[0], nexts[h], s_h.at[h], r_h.at[h], back)
        halo.start()
        halos.append(halo)

    def merged(blocks):
        if PIECES == 2:
            return blocks
        return [jnp.concatenate(blocks[i : i + 2], axis=0) for i in (0, 2)]

    def fill(s, here, after):
        total = None
        at = pl.multiple_of(s * SPAN, SPAN)
        here, after = merged(here), merged(after)
        for h in range(2):
            wide = here[h].astype(F32)
            square = jnp.sum(wide * wide, axis=0, keepdims=True)
            total = square if h == 0 else total + square
            joined = jnp.concatenate([here[h], after[h]], axis=1)
            for p in range(4):
                row = p * CH + h * 16
                phases[row : row + 16, pl.ds(at, SPAN)] = left(joined, SUB * p)[:, :SPAN]
        power[pl.ds(s, 1), :] = total

    @pl.loop(0, PLANE - 1)
    def _(s):
        fill(s, [r[s] for r in recs], [r[s + 1, :, 0:128] for r in recs])

    for halo in halos:
        halo.wait_recv()
    inside = (zh < 3).astype(F32)
    follow = [(n[...].astype(F32) * inside).astype(BF16) for n in nexts]
    fill(PLANE - 1, [r[PLANE - 1] for r in recs], [f[:, 0:128] for f in follow])
    fill(PLANE, follow, [jnp.zeros((ROWS, 128), BF16)] * PIECES)
    for h in range(PIECES):
        settle(recs[h], PLANE - 1, s_xy.at[h], r_xy.at[h], beside).wait_send()
        settle(pickss[h], 3, s_z.at[h], r_z.at[h], above).wait_send()

    double = jnp.concatenate([power[0:PLANE, :], power[1 : PLANE + 1, :]], axis=1)
    sums = {1: double}
    for size in (1, 2, 4, 8, 16, 32, 64, 128):
        sums[2 * size] = sums[size] + left(sums[size], size)
    energy = sums[256][:, :SPAN]
    start = 256
    for size in (128, 64, 32, 16, 4):
        energy = energy + left(sums[size], start)[:, :SPAN]
        start += size
    for s in range(PLANE):
        for i in range(4):
            side[s, i : i + 1, :] = energy[s : s + 1, 128 * i : 128 * i + 128]

    row = lax.broadcasted_iota(jnp.int32, (256, 256), 0)
    col = lax.broadcasted_iota(jnp.int32, (256, 256), 1)
    order = (lax.rem(row, 8) * SUB + lax.div(row, 8) == col).astype(F32).astype(BF16)
    group = lax.div(lax.broadcasted_iota(jnp.int32, (16, 128), 1), SUB).astype(F32).astype(BF16)
    for h in range(2):
        for k in range(h * PIECES // 2, (h + 1) * PIECES // 2):
            settle(tmpls[k], 3, s_g.at[k], r_g.at[k], above).wait_recv()
        for half in range(2):
            for m in range(4):
                pieces = [
                    jnp.concatenate(
                        [
                            t[(4 * half + i) // 2, i % 2, :, 128 * m : 128 * m + 128]
                            for t in tmpls[h * PIECES // 2 : (h + 1) * PIECES // 2]
                        ],
                        axis=0,
                    )
                    for i in range(4)
                ]
                for p in range(4):
                    tile = left(pieces[0], SUB * p)
                    for i in range(1, 4):
                        tile = jnp.where(group == i, left(pieces[i], SUB * (p - i) % 128), tile)
                    at = (4 * m + p) * CH + 16 * h
                    taps[at : at + 16, 128 * half : 128 * half + 128] = tile
    weights = lax.dot_general(
        order, taps[...], (((1,), (1,)), ((), ())), preferred_element_type=F32
    ).astype(BF16)

    def tell():
        spread = lax.broadcasted_iota(jnp.int32, (1, 128), 1)
        norms = jnp.zeros((1, 128), F32)
        for j in range(EVENTS):
            both = [t[j // 2, j % 2].astype(F32) for t in tmpls]
            norm = jnp.sum(sum(b * b for b in both), keepdims=True)
            norms = jnp.where(spread == j, norm, norms)
        rest = jnp.concatenate([norms, jnp.zeros((3, 128), F32)], axis=0)
        for s in range(PLANE):
            side[s, 4:8, :] = rest
        for by in flat:
            to = moved(me, by)
            there = spot(to, ("y", "x"))
            remote(side.at[there], sides.at[here], s_e, r_e, to).start()
        sides[here] = side[here]

    near = steps(("zl", "core"))
    mine = spot(me, ("zl", "core"))

    products = (product0, product1)
    turns = [lax.rem(me["y"] + d, 4) for d in (2, 1, 3, 0)]

    def multiply(i):
        at = pl.multiple_of(turns[i] * CHUNK, CHUNK)
        stack = jnp.concatenate([phases[:, pl.ds(at + 128 * m, CHUNK + 128)] for m in range(4)], axis=0)
        products[i % 2][...] = jnp.dot(weights, stack, preferred_element_type=F32)

    multiply(0)
    for i in range(4):
        if i < 3:
            multiply(i + 1)
        product = products[i % 2]
        total = product[0:8, 0:CHUNK]
        for b in range(1, SUB):
            total = total + left(product[8 * b : 8 * b + 8, :], b)[:, :CHUNK]
        for q in range(4):
            part[turns[i] * 4 + q] = total[:, SPAN * q : SPAN * q + SPAN]
        for dx in (2, 1, 3, 0):
            if i == 3 and dx == 0:
                continue
            to = {"y": turns[i], "x": lax.rem(me["x"] + dx, 4)}
            there = spot(to, ("y", "x"))
            remote(part.at[there], arrived.at[here], s_p, r_p, to).start()
        if i == 0:
            tell()
    settle(sides, PLANE - 1, s_e, r_e, beside).wait_recv()
    corner[mine] = jnp.sum(sides[...], axis=0)
    for by in near:
        remote(corner.at[mine], corner.at[mine], s_c, r_c, moved(me, by)).start()
    arrived[here] = part[here]
    settle(arrived, PLANE - 1, s_p, r_p, beside).wait_recv()

    quad[mine] = jnp.sum(arrived[...], axis=0)
    for by in near[::-1]:
        remote(quad.at[mine], quad.at[mine], s_q, r_q, moved(me, by)).start()
    partner = moved(me, near[0])
    settle(corner, 3, s_c, r_c, partner).wait_recv()
    ends = (corner[0] + corner[1]) + (corner[2] + corner[3])
    energy = jnp.concatenate([ends[i : i + 1, :] for i in range(4)], axis=1)
    row = lax.broadcasted_iota(jnp.int32, (EVENTS, 128), 0)
    col = lax.broadcasted_iota(jnp.int32, (EVENTS, 128), 1)
    norm = jnp.sum(jnp.where(row == col, ends[4:5, :], 0.0), axis=1, keepdims=True)
    root = jnp.sqrt(energy * norm + 1e-6)
    settle(sides, PLANE - 1, s_e, r_e, beside).wait_send()
    settle(arrived, PLANE - 1, s_p, r_p, beside).wait_send()
    settle(corner, 3, s_c, r_c, partner).wait_send()
    for h in range(PIECES):
        settle(tmpls[h], 3, s_g.at[h], r_g.at[h], above).wait_send()
        halos[h].wait_send()
    settle(quad, 3, s_q, r_q, partner).wait_recv()
    total = (quad[0] + quad[1]) + (quad[2] + quad[3])
    for i in range(4):
        score_ref[i] = total[2 * i : 2 * i + 2, :]
        root_ref[i] = root[2 * i : 2 * i + 2, :]
    settle(quad, 3, s_q, r_q, partner).wait_send()


def pinned(x):
    return pltpu.with_memory_space_constraint(x, pltpu.HBM)


def local(record, event_stretch, event_offset):
    dma = pltpu.SemaphoreType.DMA
    blocks = pltpu.VMEM((PLANE, ROWS, SPAN), BF16)
    pairs = pltpu.VMEM((4, 2, ROWS, SPAN), BF16)
    total, root = pl.pallas_call(
        kernel,
        out_shape=(jax.ShapeDtypeStruct((4, 2, SPAN), F32),) * 2,
        in_specs=[pl.BlockSpec(memory_space=pltpu.HBM)] * 3,
        out_specs=(pl.BlockSpec(memory_space=pltpu.VMEM),) * 2,
        scratch_shapes=[blocks] * PIECES
        + [pltpu.VMEM((ROWS, SPAN), BF16)] * PIECES
        + [pairs] * (3 * PIECES)
        + [
            pltpu.VMEM((4 * CH, (PLANE + 1) * SPAN), BF16),
            pltpu.VMEM((SPAN, 256), BF16),
            pltpu.VMEM((256, CHUNK + 128), F32),
            pltpu.VMEM((256, CHUNK + 128), F32),
            pltpu.VMEM((24, SPAN), F32),
            pltpu.VMEM((PLANE, EVENTS, SPAN), F32),
            pltpu.VMEM((PLANE, EVENTS, SPAN), F32),
            pltpu.VMEM((4, EVENTS, SPAN), F32),
            pltpu.VMEM((PLANE, EVENTS, 128), F32),
            pltpu.VMEM((PLANE, EVENTS, 128), F32),
            pltpu.VMEM((4, EVENTS, 128), F32),
        ]
        + [dma((PIECES,))] * 9
        + [dma] * 8
        + [pltpu.SMEM((2, 4), jnp.int32)] * 2
        + [dma((2,)), pltpu.VMEM((PLANE, CH, SPAN), BF16), dma],
        compiler_params=pltpu.CompilerParams(vmem_limit_bytes=56377244, collective_id=0, has_side_effects=True),
        name="matching",
    )(pinned(event_stretch.T), pinned(event_offset.T), record.reshape(PLANE, CH, SPAN))
    return total / root


def solution(mesh):
    torus = Mesh(mesh.devices.reshape(4, 4, 4, 2, 2), AXES)
    return jax.shard_map(
        local,
        mesh=torus,
        in_specs=(P(("zl", "core"), ("zh", "y", "x")), P(), P()),
        out_specs=P(None, None, ("zh", "y", "x")),
        check_vma=False,
    )
```
